32 devices in a mesh: shard: 4 (over y, x), ctx: 2 (over core), tp: 4 (over z).
Axes of the slice: x: 2, y: 2, z: 4, core: 2. Of those that a mesh axis runs over, the one named last changes fastest.
Arguments:
- hidden_in: bfloat16 [4, 2048, 2048], P('shard', 'ctx'), may hold values from -6 to 6
- doc_span: int32 [2, 4, 2048], P(None, 'shard', 'ctx'), may hold values from 0 to 2047, as said below
- cotangent: bfloat16 [4, 2048, 2048], P('shard', 'ctx'), may hold values from -6 to 6
- w_query: float32 [2048, 2048], P(('shard', 'ctx'), 'tp'), may hold values from -0.1875 to 0.1875
- w_key: float32 [2048, 2048], P(('shard', 'ctx'), 'tp'), may hold values from -0.1875 to 0.1875
- w_value: float32 [2048, 2048], P(('shard', 'ctx'), 'tp'), may hold values from -0.125 to 0.125
- w_out: float32 [2048, 2048], P('tp', ('shard', 'ctx')), may hold values from -0.75 to 0.75
- w_inner: float32 [2048, 8192], P(('shard', 'ctx'), 'tp'), may hold values from -0.125 to 0.125
- w_outer: float32 [8192, 2048], P('tp', ('shard', 'ctx')), may hold values from -0.0625 to 0.0625
- norm_gains: float32 [2, 2048], replicated, may hold values from 0.5 to 1.5
- norm_biases: float32 [2, 2048], replicated, may hold values from -1.25 to 1.25
- mom_query: float32 [2048, 2048], P(('shard', 'ctx'), 'tp'), may hold values from -112 to 112
- mom_key: float32 [2048, 2048], P(('shard', 'ctx'), 'tp'), may hold values from -112 to 112
- mom_value: float32 [2048, 2048], P(('shard', 'ctx'), 'tp'), may hold values from -112 to 112
- mom_out: float32 [2048, 2048], P('tp', ('shard', 'ctx')), may hold values from -112 to 112
- mom_inner: float32 [2048, 8192], P(('shard', 'ctx'), 'tp'), may hold values from -112 to 112
- mom_outer: float32 [8192, 2048], P('tp', ('shard', 'ctx')), may hold values from -112 to 112
- gain_moment: float32 [2, 2048], replicated, may hold values from -512 to 512
- bias_moment: float32 [2, 2048], replicated, may hold values from -512 to 512
Outputs:
- layer_out: bfloat16 [4, 2048, 2048], P('shard', 'ctx')
- input_grad: float32 [4, 2048, 2048], P('shard', 'ctx')
- grad_query: float32 [2048, 2048], P(('shard', 'ctx'), 'tp')
- grad_key: float32 [2048, 2048], P(('shard', 'ctx'), 'tp')
- grad_value: float32 [2048, 2048], P(('shard', 'ctx'), 'tp')
- grad_out: float32 [2048, 2048], P('tp', ('shard', 'ctx'))
- grad_inner: float32 [2048, 8192], P(('shard', 'ctx'), 'tp')
- grad_outer: float32 [8192, 2048], P('tp', ('shard', 'ctx'))
- gain_grad: float32 [2, 2048], replicated
- bias_grad: float32 [2, 2048], replicated
- moment_query: float32 [2048, 2048], P(('shard', 'ctx'), 'tp')
- moment_key: float32 [2048, 2048], P(('shard', 'ctx'), 'tp')
- moment_value: float32 [2048, 2048], P(('shard', 'ctx'), 'tp')
- moment_out: float32 [2048, 2048], P('tp', ('shard', 'ctx'))
- moment_inner: float32 [2048, 8192], P(('shard', 'ctx'), 'tp')
- moment_outer: float32 [8192, 2048], P('tp', ('shard', 'ctx'))
- gain_moment_new: float32 [2, 2048], replicated
- bias_moment_new: float32 [2, 2048], replicated
- new_query: float32 [2048, 2048], P(('shard', 'ctx'), 'tp')
- new_key: float32 [2048, 2048], P(('shard', 'ctx'), 'tp')
- new_value: float32 [2048, 2048], P(('shard', 'ctx'), 'tp')
- new_out: float32 [2048, 2048], P('tp', ('shard', 'ctx'))
- new_inner: float32 [2048, 8192], P(('shard', 'ctx'), 'tp')
- new_outer: float32 [8192, 2048], P('tp', ('shard', 'ctx'))
- new_gains: float32 [2, 2048], replicated
- new_biases: float32 [2, 2048], replicated
The draws below stay inside these ranges and needn't reach their ends.
Inputs may be any that keep to these rules, and one draw needn't show every extreme that they name: doc_span[0, r, i] <= i <= doc_span[1, r, i]; the positions of a packed row that share one pair form a run of consecutive positions (a document), and the documents of a row follow one another without gaps.
All inputs are finite; a program needn't handle non-finite values.
Results may differ from the reference program's by a relative error of at most 0.014.
The reference program's roundings to bfloat16 on the way count: a program that leaves them out, or rounds other values in their place, can miss the bound.
Values may be sent and summed in bfloat16 or wider, within the bound.
No kernel may reach another device: no remote copies, remote signals or barrier semaphores. Data moves between devices by JAX's collectives and lax.ppermute only.
A program may use at most 256 MiB of HBM per device.

```python
import jax
import jax.numpy as jnp
from jax import lax

D = 2048
HEADS = 16
HEAD_DIM = 128
FF = 8192
TOK_DEV = 1024
REACH = 512
BW = 512
NS_STEPS = 5
ROWS = 4
LEN = 2048
TOKENS = 8192


def draw_doc_span(key, part):
    doc_marks = jax.random.randint(key, (ROWS, LEN), 0, REACH) == 0
    position = jnp.broadcast_to(jnp.arange(LEN, dtype=jnp.int32)[None, :], (ROWS, LEN))
    opening = doc_marks | (position == 0)
    closing = jnp.concatenate([opening[:, 1:], jnp.ones((ROWS, 1), dtype=jnp.bool_)], axis=1)
    first_pos = lax.cummax(jnp.where(opening, position, 0), axis=1)
    last_pos = lax.cummin(jnp.where(closing, position, LEN - 1), axis=1, reverse=True)
    return jnp.stack([first_pos, last_pos]).astype(jnp.int32)


def block_scale(stream_key, shape, cuts, low, largest):
    loudness, own = 1.0, jax.random.fold_in(stream_key, 6)
    for axis_at, shards_of in cuts:
        draws = jnp.exp(jax.random.uniform(jax.random.fold_in(own, axis_at), (shards_of,), jnp.float32, low / len(cuts), largest / len(cuts)))
        loudness = loudness * jnp.repeat(draws, shape[axis_at] // shards_of).reshape([-1 if axis == axis_at else 1 for axis in range(len(shape))])
    return loudness


def gaussian(rng, extent, scale, bound, split=(), kind=jnp.bfloat16):
    drawn = jax.random.normal(rng, extent, jnp.float32) * scale
    if len(split) > 0:
        drawn = block_scale(rng, extent, split, -0.22, 0.18) * drawn
    return jnp.clip(drawn, min=-bound, max=bound).astype(kind)


def setup_inputs(seed: int = 0) -> dict:
    key_list = jax.random.split(jax.random.key(seed), 20)
    return {
        "hidden_in": gaussian(key_list[0], (ROWS, LEN, D), 1.0, 6.0, ((0, 4), (1, 2))),
        "doc_span": draw_doc_span(jax.random.fold_in(key_list[19], 71), 0),
        "cotangent": gaussian(key_list[2], (ROWS, LEN, D), 1.0, 6.0, ((0, 4), (1, 2))),
        "w_query": gaussian(key_list[3], (D, D), (D // 2) ** -0.5, 0.1875, ((0, 8), (1, 4)), jnp.float32),
        "w_key": gaussian(key_list[4], (D, D), (D // 2) ** -0.5, 0.1875, ((0, 8), (1, 4)), jnp.float32),
        "w_value": gaussian(key_list[5], (D, D), D ** -0.5, 0.125, ((0, 8), (1, 4)), jnp.float32),
        "w_out": gaussian(key_list[6], (D, D), (D // 32) ** -0.5, 0.75, ((0, 4), (1, 8)), jnp.float32),
        "w_inner": gaussian(key_list[7], (D, FF), D ** -0.5, 0.125, ((0, 8), (1, 4)), jnp.float32),
        "w_outer": gaussian(key_list[8], (FF, D), FF ** -0.5, 0.0625, ((0, 4), (1, 8)), jnp.float32),
        "norm_gains": jnp.clip(1.0 + 0.1 * jax.random.normal(key_list[9], (2, D), jnp.float32), 0.5, 1.5),
        "norm_biases": gaussian(key_list[10], (2, D), 0.2, 1.25, (), jnp.float32),
        "mom_query": gaussian(key_list[11], (D, D), (0.2 * (ROWS * LEN) ** 0.5), 112.0, ((0, 8), (1, 4)), jnp.float32),
        "mom_key": gaussian(key_list[12], (D, D), (0.2 * (ROWS * LEN) ** 0.5), 112.0, ((0, 8), (1, 4)), jnp.float32),
        "mom_value": gaussian(key_list[13], (D, D), (0.2 * (ROWS * LEN) ** 0.5), 112.0, ((0, 8), (1, 4)), jnp.float32),
        "mom_out": gaussian(key_list[14], (D, D), (0.2 * (ROWS * LEN) ** 0.5), 112.0, ((0, 4), (1, 8)), jnp.float32),
        "mom_inner": gaussian(key_list[15], (D, FF), (0.2 * (ROWS * LEN) ** 0.5), 112.0, ((0, 8), (1, 4)), jnp.float32),
        "mom_outer": gaussian(key_list[16], (FF, D), (0.2 * (ROWS * LEN) ** 0.5), 112.0, ((0, 4), (1, 8)), jnp.float32),
        "gain_moment": gaussian(key_list[17], (2, D), ((ROWS * LEN) ** 0.5), 512.0, (), jnp.float32),
        "bias_moment": gaussian(key_list[18], (2, D), ((ROWS * LEN) ** 0.5), 512.0, (), jnp.float32),
    }


@jax.custom_vjp
def low(v):
    return lax.optimization_barrier(v.astype(jnp.bfloat16)).astype(jnp.float32)

@jax.custom_vjp
def low_back(v):
    return v

def low_keep(v):
    return (low(v), None)

def low_pass(kept, grad):
    return (grad,)

def back_keep(v):
    return (v, None)

def back_low(kept, grad):
    return (low(grad),)
low.defvjp(low_keep, low_pass)
low_back.defvjp(back_keep, back_low)
NS_COEFFS = (3.4445, -4.775, 2.0315)
LN_EPSILON = 1e-12
BETA = 0.5
MATRIX_RATE = 0.5
VECTOR_RATE = 0.3
MASKED = -1e+30

def product(left, right):
    return jnp.dot(left, right, precision=lax.Precision.HIGHEST, preferred_element_type=jnp.float32)

def layer_norm(hidden, gain, shift):
    centred = hidden - lax.optimization_barrier(jnp.mean(hidden, axis=-1, keepdims=True))
    variance = lax.optimization_barrier(jnp.mean(centred * centred, axis=-1, keepdims=True))
    return centred * lax.rsqrt(variance + LN_EPSILON) * gain + shift

def gelu_tanh(values):
    return jax.nn.gelu(values, approximate=True)

def attention(queries, keys, values, doc_bounds):
    block_rows = min(512, TOK_DEV)
    key_span = block_rows + 2 * REACH
    padded_keys = jnp.pad(keys, ((REACH, REACH), (0, 0), (0, 0)))
    padded_values = jnp.pad(values, ((REACH, REACH), (0, 0), (0, 0)))

    def one_block(block_index):
        offset = block_index * block_rows
        query_rows = lax.dynamic_slice_in_dim(queries, offset, block_rows, 0)
        key_rows = lax.dynamic_slice_in_dim(padded_keys, offset, key_span, 0)
        value_rows = lax.dynamic_slice_in_dim(padded_values, offset, key_span, 0)
        lower = lax.dynamic_slice_in_dim(doc_bounds[0], offset, block_rows, 0)
        upper = lax.dynamic_slice_in_dim(doc_bounds[1], offset, block_rows, 0)
        query_pos = offset + jnp.arange(block_rows, dtype=jnp.int32)
        key_pos = offset - REACH + jnp.arange(key_span, dtype=jnp.int32)
        visible = (key_pos[None, :] >= lower[:, None]) & (key_pos[None, :] <= upper[:, None])
        visible = visible & (jnp.abs(key_pos[None, :] - query_pos[:, None]) <= REACH)
        raw = jnp.einsum('ihd,jhd->hij', query_rows, key_rows, precision=lax.Precision.HIGHEST)
        scores = jnp.where(visible[None], low_back(raw) * HEAD_DIM ** (-0.5), MASKED)
        row_max = lax.optimization_barrier(jnp.max(scores, axis=-1, keepdims=True))
        expo = jnp.exp(scores - row_max)
        probabilities = low(expo / lax.optimization_barrier(jnp.sum(expo, axis=-1, keepdims=True)))
        return jnp.einsum('hij,jhd->ihd', probabilities, value_rows, precision=lax.Precision.HIGHEST)
    blocks = lax.map(jax.checkpoint(one_block), jnp.arange(LEN // block_rows, dtype=jnp.int32))
    return blocks.reshape(LEN, HEADS * HEAD_DIM)

def row_forward(params, hidden, doc_bounds):
    w_query, w_key, w_value, w_out, w_inner, w_outer, gains, biases = params
    head_shape = (LEN, HEADS, HEAD_DIM)
    queries = low(low_back(product(hidden, low(w_query)))).reshape(head_shape)
    keys_all = low(low_back(product(hidden, low(w_key)))).reshape(head_shape)
    values_all = low(low_back(product(hidden, low(w_value)))).reshape(head_shape)
    attended = low(low_back(attention(queries, keys_all, values_all, doc_bounds)))
    branch = low_back(product(attended, low(w_out)))
    normed = layer_norm(hidden + branch, gains[0], biases[0])
    pre_act = low_back(product(low(normed), low(w_inner)))
    ffn_branch = low_back(product(low(gelu_tanh(pre_act)), low(w_outer)))
    return layer_norm(normed + ffn_branch, gains[1], biases[1])

def orthogonalize(block):
    iterate = block / (jnp.sqrt(jnp.sum(block * block)) + 1e-07)
    for step_index in range(NS_STEPS):
        gram = product(iterate.T, iterate)
        polynomial = NS_COEFFS[1] * gram + NS_COEFFS[2] * product(gram, gram)
        iterate = NS_COEFFS[0] * iterate + product(iterate, polynomial)
    return iterate

def orthogonal_columns(matrix):
    column_blocks = matrix.shape[1] // BW
    blocks = jnp.transpose(matrix.reshape(D, column_blocks, BW), (1, 0, 2))
    finished = lax.map(orthogonalize, blocks)
    return jnp.transpose(finished, (1, 0, 2)).reshape(D, column_blocks * BW)

def reference(hidden_in, doc_span, cotangent, w_query, w_key, w_value, w_out, w_inner, w_outer, norm_gains, norm_biases, mom_query, mom_key, mom_value, mom_out, mom_inner, mom_outer, gain_moment, bias_moment):
    params = (w_query, w_key, w_value, w_out, w_inner, w_outer, norm_gains, norm_biases)

    def one_row(totals, inputs):
        hidden, doc_bounds, seed_grad = inputs
        result, pullback = jax.vjp(lambda weights, acts: row_forward(weights, acts, doc_bounds), params, hidden.astype(jnp.float32))
        weight_grads, hidden_grad = pullback(seed_grad.astype(jnp.float32))
        totals = jax.tree.map(jnp.add, totals, weight_grads)
        return (totals, (result.astype(jnp.bfloat16), hidden_grad))
    initial = jax.tree.map(jnp.zeros_like, params)
    all_grads, outputs = lax.scan(one_row, initial, (hidden_in, jnp.moveaxis(doc_span, 1, 0), cotangent))
    layer_out, input_grad = outputs
    grad_query, grad_key, grad_value, grad_out, grad_inner, grad_outer, gain_grad, bias_grad = all_grads
    moment_query = BETA * mom_query + (1.0 - BETA) * grad_query
    moment_key = BETA * mom_key + (1.0 - BETA) * grad_key
    moment_value = BETA * mom_value + (1.0 - BETA) * grad_value
    moment_out = BETA * mom_out + (1.0 - BETA) * grad_out
    moment_inner = BETA * mom_inner + (1.0 - BETA) * grad_inner
    moment_outer = BETA * mom_outer + (1.0 - BETA) * grad_outer
    gain_moment_new = BETA * gain_moment + (1.0 - BETA) * gain_grad
    bias_moment_new = BETA * bias_moment + (1.0 - BETA) * bias_grad
    new_query = w_query - MATRIX_RATE * orthogonal_columns(moment_query)
    new_key = w_key - MATRIX_RATE * orthogonal_columns(moment_key)
    new_value = w_value - MATRIX_RATE * orthogonal_columns(moment_value)
    new_out = w_out - MATRIX_RATE * orthogonal_columns(moment_out.T).T
    new_inner = w_inner - MATRIX_RATE * orthogonal_columns(moment_inner)
    new_outer = w_outer - MATRIX_RATE * orthogonal_columns(moment_outer.T).T
    new_gains = norm_gains - VECTOR_RATE * gain_moment_new / TOKENS ** 0.5
    new_biases = norm_biases - VECTOR_RATE * bias_moment_new / TOKENS ** 0.5
    return (layer_out, input_grad, grad_query, grad_key, grad_value, grad_out, grad_inner, grad_outer, gain_grad, bias_grad, moment_query, moment_key, moment_value, moment_out, moment_inner, moment_outer, gain_moment_new, bias_moment_new, new_query, new_key, new_value, new_out, new_inner, new_outer, new_gains, new_biases)
```

```python
import functools
import math

import jax
import jax.numpy as jnp
from jax import lax
from jax.experimental import pallas as pl
from jax.experimental.pallas import tpu as pltpu
from jax.sharding import PartitionSpec as P

HEAD_DIM = 128
REACH = 512
BW = 512
NS_STEPS = 5
QUERY_ROWS = 256

NS_COEFFS = (3.4445, -4.775, 2.0315)
LN_EPSILON = 1e-12
BETA = 0.5
MATRIX_RATE = 0.5
VECTOR_RATE = 0.3
MASKED = -1e30
WEIGHT_AXES = ("shard", "ctx")
BF16 = jnp.bfloat16
F32 = jnp.float32


def upward(first, last):
    return [(i, i + 1) for i in range(first, last)]


def downward(first, last):
    return [(i, i - 1) for i in range(first, last)]


def ring(count, by):
    return [(i, (i + by) % count) for i in range(count)]


def spread(block, axis):
    count = lax.axis_size(axis)
    return [block] + [lax.ppermute(block, axis, ring(count, r)) for r in range(1, count)]


def send_slot(block, axis, r):
    return lax.ppermute(block, axis, ring(lax.axis_size(axis), -r))


def slot_order(count):
    return sorted(range(1, count), key=lambda r: (-min(r, count - r), r)) + [0]


def total_over(value, axes):
    for axis in axes:
        by = 1
        while by < lax.axis_size(axis):
            pairs = [(i, i ^ by) for i in range(lax.axis_size(axis))]
            value = value + lax.ppermute(value, axis, pairs)
            by *= 2
    return value


def after(value, *others):
    return lax.optimization_barrier((value, *others))[0]


def dot(left, right):
    return jnp.dot(left, right, preferred_element_type=F32)


def dot_nt(left, right):
    return lax.dot_general(left, right, (((1,), (1,)), ((), ())), preferred_element_type=F32)


def dot_tn(left, right):
    return lax.dot_general(left, right, (((0,), (0,)), ((), ())), preferred_element_type=F32)


def normalize(hidden):
    centred = hidden - jnp.mean(hidden, axis=-1, keepdims=True)
    variance = jnp.mean(centred * centred, axis=-1, keepdims=True)
    scale = lax.rsqrt(variance + LN_EPSILON)
    return centred * scale, scale


def norm_backward(grad, unit, scale, gain):
    scaled = grad * gain
    inner = jnp.mean(scaled * unit, axis=-1, keepdims=True)
    dhidden = scale * (scaled - jnp.mean(scaled, axis=-1, keepdims=True) - unit * inner)
    return dhidden, jnp.sum(grad * unit, axis=0), jnp.sum(grad, axis=0)


def gelu_tanh(values):
    return jax.nn.gelu(values, approximate=True)


def window_probs(q, keys, low_ref, high_ref, start):
    scores = dot_nt(keys, q) * (HEAD_DIM**-0.5)
    at = start + lax.broadcasted_iota(jnp.int32, scores.shape, 0)
    scores = jnp.where((at >= low_ref[...]) & (at <= high_ref[...]), scores, MASKED)
    expo = jnp.exp(scores - jnp.max(scores, axis=0, keepdims=True))
    return expo * (1.0 / jnp.sum(expo, axis=0, keepdims=True))


def attend_kernel(low_ref, high_ref, q_ref, k_ref, v_ref, o_ref):
    rows = q_ref.shape[0]
    span = rows + 2 * REACH
    start = pl.multiple_of(pl.program_id(1) * rows, rows)
    probs = window_probs(q_ref[...], k_ref[pl.ds(start, span), :], low_ref, high_ref, start)
    o_ref[...] = dot_tn(probs.astype(BF16), v_ref[pl.ds(start, span), :]).astype(BF16)


def attend_back_kernel(low_ref, high_ref, q_ref, k_ref, v_ref, g_ref, dq_ref, dk_ref, dv_ref):
    rows = q_ref.shape[0]
    span = rows + 2 * REACH
    start = pl.multiple_of(pl.program_id(1) * rows, rows)
    window = pl.ds(start, span)

    @pl.when(pl.program_id(1) == 0)
    def _():
        dk_ref[...] = jnp.zeros_like(dk_ref)
        dv_ref[...] = jnp.zeros_like(dv_ref)

    q, g, keys = q_ref[...], g_ref[...], k_ref[window, :]
    probs = window_probs(q, keys, low_ref, high_ref, start)
    dprobs = dot_nt(v_ref[window, :], g)
    offset = jnp.sum(dprobs * probs, axis=0, keepdims=True)
    dscores = (probs * (dprobs - offset) * (HEAD_DIM**-0.5)).astype(BF16)
    dv_ref[window, :] += dot(probs.astype(BF16), g)
    dk_ref[window, :] += dot(dscores, q)
    dq_ref[...] = dot_tn(dscores, keys).astype(BF16)


def attention_specs(rows, padded, heads):
    bounds = pl.BlockSpec((1, rows), lambda h, b: (0, b))
    queries = pl.BlockSpec((rows, HEAD_DIM), lambda h, b: (b, h))
    keys = pl.BlockSpec((padded, HEAD_DIM), lambda h, b: (0, h))
    values = pl.BlockSpec((padded, HEAD_DIM), lambda h, b: (0, h + heads))
    return bounds, queries, keys, values


def attend(low, high, queries, padded_kv, heads):
    length, padded = queries.shape[0], padded_kv.shape[0]
    rows = min(QUERY_ROWS, length)
    bounds, q_spec, k_spec, v_spec = attention_specs(rows, padded, heads)
    pairs = heads * length * (rows + 2 * REACH)
    return pl.pallas_call(
        attend_kernel,
        grid=(heads, length // rows),
        in_specs=[bounds, bounds, q_spec, k_spec, v_spec],
        out_specs=q_spec,
        out_shape=jax.ShapeDtypeStruct((length, heads * HEAD_DIM), BF16),
        cost_estimate=pl.CostEstimate(
            flops=16 * pairs * HEAD_DIM, transcendentals=pairs, bytes_accessed=8 << 20
        ),
        name="attend",
    )(low, high, queries, padded_kv, padded_kv)


def attend_back(low, high, queries, padded_kv, grads, heads):
    length, padded = queries.shape[0], padded_kv.shape[0]
    rows = min(QUERY_ROWS, length)
    bounds, q_spec, k_spec, v_spec = attention_specs(rows, padded, heads)
    pairs = heads * length * (rows + 2 * REACH)
    total = jax.ShapeDtypeStruct((padded, heads * HEAD_DIM), F32)
    return pl.pallas_call(
        attend_back_kernel,
        grid=(heads, length // rows),
        in_specs=[bounds, bounds, q_spec, k_spec, v_spec, q_spec],
        out_specs=(q_spec, k_spec, k_spec),
        out_shape=(jax.ShapeDtypeStruct((length, heads * HEAD_DIM), BF16), total, total),
        cost_estimate=pl.CostEstimate(
            flops=32 * pairs * HEAD_DIM, transcendentals=pairs, bytes_accessed=20 << 20
        ),
        name="attend_back",
    )(low, high, queries, padded_kv, padded_kv, grads)


def halves(value):
    top = value.astype(BF16)
    return top, (value - top.astype(F32)).astype(BF16)


def newton_schulz_kernel(block_ref, out_ref, iterate, top, rest):
    depth, width = block_ref.shape
    chunk = min(256, depth)
    chunks = depth // chunk

    def columns(c):
        return pl.ds(pl.multiple_of(c * chunk, chunk), chunk)

    def load(c, total):
        part = block_ref[columns(c), :].astype(F32)
        iterate[:, columns(c)] = part.T
        return total + jnp.sum(part * part, axis=(0, 1), keepdims=True)

    norm = jnp.sqrt(lax.fori_loop(0, chunks, load, jnp.zeros((1, 1), F32)))
    inverse = 1.0 / (norm + 1e-07)

    def split(c, scale):
        value = iterate[:, columns(c)] * scale
        iterate[:, columns(c)] = value
        top[:, columns(c)], rest[:, columns(c)] = halves(value)
        return scale

    lax.fori_loop(0, chunks, split, inverse)

    def step(index, carry):
        cross = dot_nt(rest[...], top[...])
        gram = dot_nt(top[...], top[...]) + (cross + cross.T)
        gram_top, gram_rest = halves(gram)
        cross = dot(gram_top, gram_rest)
        square = dot(gram_top, gram_top) + (cross + cross.T)
        poly_top, poly_rest = halves(NS_COEFFS[1] * gram + NS_COEFFS[2] * square)

        def update(c, carry):
            here = columns(c)
            change = dot(poly_top, top[:, here]) + dot(poly_rest, top[:, here])
            value = NS_COEFFS[0] * iterate[:, here] + (change + dot(poly_top, rest[:, here]))
            iterate[:, here] = value
            top[:, here], rest[:, here] = halves(value)
            return carry

        return lax.fori_loop(0, chunks, update, carry)

    lax.fori_loop(0, NS_STEPS, step, 0)

    def store(c, carry):
        out_ref[columns(c), :] = iterate[:, columns(c)].T.astype(BF16)
        return carry

    lax.fori_loop(0, chunks, store, 0)


def newton_schulz(block):
    depth, width = block.shape
    return pl.pallas_call(
        newton_schulz_kernel,
        out_shape=jax.ShapeDtypeStruct((depth, width), BF16),
        in_specs=[pl.BlockSpec(memory_space=pltpu.VMEM)],
        out_specs=pl.BlockSpec(memory_space=pltpu.VMEM),
        scratch_shapes=[
            pltpu.VMEM((width, depth), F32),
            pltpu.VMEM((width, depth), BF16),
            pltpu.VMEM((width, depth), BF16),
        ],
        cost_estimate=pl.CostEstimate(
            flops=2 * NS_STEPS * width * width * (5 * depth + 2 * width),
            transcendentals=0,
            bytes_accessed=4 * depth * width,
        ),
        name="newton_schulz",
    )(block)


def orthogonal_blocks(blocks):
    group = lax.axis_size("shard") * lax.axis_size("ctx")
    copies = group // len(blocks)
    sent = jnp.stack([block.astype(BF16) for block in blocks for _ in range(copies)])
    owned = lax.all_to_all(sent, WEIGHT_AXES, split_axis=0, concat_axis=0, tiled=True)
    done = newton_schulz(owned.reshape(-1, BW)).reshape(owned.shape)
    back = lax.all_to_all(done, WEIGHT_AXES, split_axis=0, concat_axis=0, tiled=True)
    return [back[b * copies].astype(F32) for b in range(len(blocks))]


def column_blocks(value):
    return [value[:, at : at + BW] for at in range(0, value.shape[1], BW)]


def gather_rows(value):
    return lax.all_gather(value, WEIGHT_AXES, axis=0, tiled=True)


def scatter_rows(value):
    low = value.astype(BF16)
    return lax.psum_scatter(low, WEIGHT_AXES, scatter_dimension=0, tiled=True).astype(F32)


def blend(old, grad):
    return BETA * old + (1.0 - BETA) * grad


def body(
    hidden_in,
    doc_span,
    cotangent,
    w_query,
    w_key,
    w_value,
    w_out,
    w_inner,
    w_outer,
    norm_gains,
    norm_biases,
    mom_query,
    mom_key,
    mom_value,
    mom_out,
    mom_inner,
    mom_outer,
    gain_moment,
    bias_moment,
):
    tp = lax.axis_size("tp")
    me = lax.axis_index("tp")
    hidden = hidden_in[0]
    length, width = hidden.shape
    share = length // tp
    local = w_query.shape[1]
    heads = local // HEAD_DIM

    def slice_of(value, r):
        return lax.dynamic_slice_in_dim(value, lax.rem(me - r + tp, tp) * share, share, 0)

    def in_place(slots, dtype):
        whole = jnp.zeros((length, slots[0].shape[1]), dtype)
        for r, slot in enumerate(slots):
            at = lax.rem(me - r + tp, tp) * share
            whole = lax.dynamic_update_slice_in_dim(whole, slot.astype(dtype), at, 0)
        return whole

    full_qkv = gather_rows(jnp.concatenate([w_query, w_key, w_value], axis=1).astype(BF16))
    out_slots = spread(w_out.T.astype(BF16), "tp")
    full_out_t = gather_rows(after(jnp.concatenate(out_slots, axis=1), full_qkv))
    full_inner = gather_rows(after(w_inner.astype(BF16), full_out_t))
    full_outer_t = gather_rows(after(w_outer.T.astype(BF16), full_inner))

    qkv = dot(hidden, full_qkv).astype(BF16)
    queries, own_kv = qkv[:, :local], qkv[:, local:]
    ctx = lax.axis_size("ctx")
    above = lax.ppermute(own_kv[length - REACH :], "ctx", upward(0, ctx - 1))
    below = lax.ppermute(own_kv[:REACH], "ctx", downward(1, ctx))
    padded_kv = jnp.concatenate([above, own_kv, below], axis=0)

    position = jnp.arange(length, dtype=jnp.int32)
    anchor = lax.axis_index("ctx") * length - REACH
    low = jnp.maximum(doc_span[0] - anchor, position[None])
    high = jnp.minimum(doc_span[1] - anchor, position[None] + 2 * REACH)
    attended = attend(low, high, queries, padded_kv, heads)

    head_slots = spread(attended, "tp")
    order = slot_order(tp)
    attended_slots, normed_slots, pre_slots, act_slots, sums = ([None] * tp for _ in range(5))
    for r in order:
        attended_slots[r] = jnp.concatenate([slice_of(slot, r) for slot in head_slots], axis=1)
        branch = dot_nt(attended_slots[r], full_out_t)
        unit, scale = normalize(slice_of(hidden, r).astype(F32) + branch)
        normed = unit * norm_gains[0] + norm_biases[0]
        normed_slots[r] = normed.astype(BF16)
        pre_slots[r] = dot(normed_slots[r], full_inner)
        act_slots[r] = gelu_tanh(pre_slots[r]).astype(BF16)
        sums[r] = dot_nt(act_slots[r], full_outer_t)
        if r:
            sums[r] = send_slot(sums[r].astype(BF16), "tp", r).astype(F32)
    unit_one, scale_one, own_normed = unit, scale, normed
    second = own_normed + sum(sums[1:], sums[0])

    unit_two, scale_two = normalize(second)
    own_out = (unit_two * norm_gains[1] + norm_biases[1]).astype(BF16)
    seed = slice_of(cotangent[0], 0).astype(F32)
    grad_two, gain_two, shift_two = norm_backward(seed, unit_two, scale_two, norm_gains[1])
    dffn_slots = spread(grad_two.astype(BF16), "tp")
    slopes = lax.optimization_barrier((*pre_slots, dffn_slots[0]))[:tp]
    slopes = [jax.vjp(gelu_tanh, pre)[1](jnp.ones_like(pre))[0] for pre in slopes]
    slopes = lax.optimization_barrier(slopes)
    dpre_slots, sums = [None] * tp, [None] * tp
    for r in order:
        dact = dot(dffn_slots[r], full_outer_t)
        dpre_slots[r] = (dact * slopes[r]).astype(BF16)
        sums[r] = dot_nt(dpre_slots[r], full_inner)
        if r:
            sums[r] = send_slot(sums[r].astype(BF16), "tp", r).astype(F32)
    act = jnp.concatenate(act_slots, axis=0)
    dffn = jnp.concatenate(dffn_slots, axis=0)
    act = after(act, *dpre_slots, sums[0])
    grad_outer_t = scatter_rows(dot_tn(dffn, act))
    normed_low = jnp.concatenate(normed_slots, axis=0)
    dpre = jnp.concatenate(dpre_slots, axis=0)
    grad_inner = scatter_rows(dot_tn(normed_low, dpre))
    dnormed = grad_two + sum(sums[1:], sums[0])

    grad_one, gain_one, shift_one = norm_backward(dnormed, unit_one, scale_one, norm_gains[0])
    dbranch_low = grad_one.astype(BF16)
    dattended_all = dot(dbranch_low, full_out_t).astype(BF16)
    dattended_slots = []
    for r in range(tp):
        sent = dattended_all[:, ((tp - r) % tp) * local : ((tp - r) % tp + 1) * local]
        if r:
            sent = lax.ppermute(sent, "tp", ring(tp, r))
        dattended_slots.append(sent)
    dattended = in_place(dattended_slots, BF16)

    part = width // tp
    dbranch_slots = []
    for r in range(tp):
        at = lax.rem(me + r, tp) * part
        sent = lax.dynamic_slice_in_dim(after(dbranch_low, dattended_all), at, part, 1)
        dbranch_slots.append(lax.ppermute(sent, "tp", ring(tp, r)) if r else sent)
    out_slots = spread(after(own_out, dattended), "tp")

    dq_low, key_grad, value_grad = attend_back(low, high, queries, padded_kv, dattended, heads)
    kv_grad = jnp.concatenate([key_grad, value_grad], axis=1)
    from_above = lax.ppermute(kv_grad[:REACH].astype(BF16), "ctx", downward(1, ctx))
    from_below = lax.ppermute(kv_grad[length + REACH :].astype(BF16), "ctx", upward(0, ctx - 1))
    centre = kv_grad[REACH : length + REACH]
    centre = centre.at[length - REACH :].add(from_above.astype(F32))
    centre = centre.at[:REACH].add(from_below.astype(F32))
    dqkv = jnp.concatenate([dq_low, centre.astype(BF16)], axis=1)
    grad_qkv = dot_tn(hidden, dqkv).astype(BF16)
    dqkv = after(dqkv, grad_qkv)
    grad_qkv = scatter_rows(grad_qkv)
    sums = [None] * tp
    for r in order:
        sums[r] = dot_nt(slice_of(dqkv, r), full_qkv)
        if r:
            sums[r] = send_slot(sums[r].astype(BF16), "tp", r).astype(F32)
    own_input_grad = grad_one + sum(sums[1:], sums[0])
    input_grad = in_place(spread(own_input_grad.astype(BF16), "tp"), F32)[None]
    layer_out = in_place(out_slots, BF16)[None]

    rows = w_query.shape[0]
    group = width // rows
    dbranch = jnp.concatenate(dbranch_slots, axis=0)
    attended_all = after(jnp.concatenate(attended_slots, axis=0), dqkv)
    pieces = dot_tn(dbranch, attended_all).astype(BF16).reshape(group // tp, rows, tp, local)
    pieces = jnp.transpose(pieces, (0, 2, 1, 3)).reshape(group * rows, local)
    piece = lax.psum_scatter(pieces, WEIGHT_AXES, scatter_dimension=0, tiled=True)
    homes = [
        (p * tp + t, (t * (group // tp) + p // tp) * tp + (t - p % tp) % tp)
        for p in range(group)
        for t in range(tp)
    ]
    grad_out_t = lax.ppermute(piece, (*WEIGHT_AXES, "tp"), homes).astype(F32)

    totals = total_over(
        jnp.stack([gain_one, gain_two, shift_one, shift_two]), ("ctx", "shard", "tp")
    )
    gain_grad, bias_grad = totals[:2], totals[2:]

    moment_inner = blend(mom_inner, grad_inner)
    moment_outer_t = blend(mom_outer.T, grad_outer_t)
    ortho = orthogonal_blocks(column_blocks(moment_inner) + column_blocks(moment_outer_t))
    half = len(ortho) // 2
    new_inner = w_inner - MATRIX_RATE * jnp.concatenate(ortho[:half], axis=1)
    new_outer = w_outer - MATRIX_RATE * jnp.concatenate(ortho[half:], axis=1).T

    grad_query, grad_key, grad_value = jnp.split(grad_qkv, 3, axis=1)
    moment_query = blend(mom_query, grad_query)
    moment_key = blend(mom_key, grad_key)
    moment_value = blend(mom_value, grad_value)
    moment_out_t = blend(mom_out.T, grad_out_t)
    ortho = orthogonal_blocks(
        sum(map(column_blocks, (moment_query, moment_key, moment_value, moment_out_t)), [])
    )
    per = len(ortho) // 4
    ortho = [jnp.concatenate(ortho[per * m : per * m + per], axis=1) for m in range(4)]
    new_query = w_query - MATRIX_RATE * ortho[0]
    new_key = w_key - MATRIX_RATE * ortho[1]
    new_value = w_value - MATRIX_RATE * ortho[2]
    new_out = w_out - MATRIX_RATE * ortho[3].T

    tokens_all = length * lax.axis_size("shard") * ctx
    gain_moment_new = blend(gain_moment, gain_grad)
    bias_moment_new = blend(bias_moment, bias_grad)
    new_gains = norm_gains - VECTOR_RATE * gain_moment_new / math.sqrt(tokens_all)
    new_biases = norm_biases - VECTOR_RATE * bias_moment_new / math.sqrt(tokens_all)
    return (
        layer_out,
        input_grad,
        grad_query,
        grad_key,
        grad_value,
        grad_out_t.T,
        grad_inner,
        grad_outer_t.T,
        gain_grad,
        bias_grad,
        moment_query,
        moment_key,
        moment_value,
        moment_out_t.T,
        moment_inner,
        moment_outer_t.T,
        gain_moment_new,
        bias_moment_new,
        new_query,
        new_key,
        new_value,
        new_out,
        new_inner,
        new_outer,
        new_gains,
        new_biases,
    )


def solution(mesh):
    tokens = P("shard", "ctx", None)
    by_rows = P(WEIGHT_AXES, "tp")
    by_columns = P("tp", WEIGHT_AXES)
    matrices = (by_rows, by_rows, by_rows, by_columns, by_rows, by_columns)
    return jax.shard_map(
        body,
        mesh=mesh,
        in_specs=(tokens, P(None, "shard", "ctx"), tokens, *matrices, P(), P(), *matrices, P(), P()),
        out_specs=(tokens, tokens, *matrices, P(), P(), *matrices, P(), P(), *matrices, P(), P()),
        check_vma=False,
    )
```

```python
import functools
import math

import jax
import jax.numpy as jnp
from jax import lax
from jax.experimental import pallas as pl
from jax.experimental.layout import Layout, with_layout_constraint
from jax.experimental.pallas import tpu as pltpu
from jax.sharding import PartitionSpec as P

HEAD_DIM = 128
REACH = 512
BW = 512
NS_STEPS = 5
QUERY_ROWS = 256

NS_COEFFS = (3.4445, -4.775, 2.0315)
LN_EPSILON = 1e-12
BETA = 0.5
MATRIX_RATE = 0.5
VECTOR_RATE = 0.3
MASKED = -1e30
WEIGHT_AXES = ("shard", "ctx")
BF16 = jnp.bfloat16
F32 = jnp.float32


def along(value, axis, pairs):
    return value, functools.partial(lax.ppermute, axis_name=axis, perm=pairs)


def upward(first, last):
    return [(i, i + 1) for i in range(first, last)]


def downward(first, last):
    return [(i, i - 1) for i in range(first, last)]


class Gather:
    def __init__(self, block, axis):
        self.count, self.axis = lax.axis_size(axis), axis
        self.block, self.ups, self.downs = block, [], []

    def sends(self):
        step = len(self.ups) + 1
        up, down = (self.ups[-1], self.downs[-1]) if self.ups else (self.block, self.block)
        return [
            along(up, self.axis, upward(step - 1, self.count - 1)),
            along(down, self.axis, downward(1, self.count - step + 1)),
        ]

    def take(self, got):
        self.ups.append(got[0])
        self.downs.append(got[1])

    def slot(self, r):
        return self.ups[r - 1] + self.downs[self.count - r - 1] if r else self.block

    def slots(self):
        return [self.slot(r) for r in range(self.count)]

    def terms(self):
        pairs = [[self.ups[r - 1], self.downs[self.count - r - 1]] for r in range(1, self.count)]
        return [[self.block], *pairs]


class Scatter:
    def __init__(self, parts, axis):
        self.count, self.axis = lax.axis_size(axis), axis
        self.parts, self.step, self.got = parts, 0, None

    def sends(self):
        self.step += 1
        step, count = self.step, self.count
        terms = [self.parts[step], self.parts[count - step]]
        if self.got:
            terms = [
                term.astype(F32) + got.astype(F32) for term, got in zip(terms, self.got)
            ]
        return [
            along(terms[0].astype(BF16), self.axis, upward(0, step)),
            along(terms[1].astype(BF16), self.axis, downward(count - step, count)),
        ]

    def take(self, got):
        self.got = got

    def total(self):
        return self.parts[0].astype(F32) + (self.got[0].astype(F32) + self.got[1].astype(F32))


class Exchange:
    def __init__(self, blocks, axis):
        self.blocks, self.axis = blocks, axis

    def sends(self):
        count = len(self.blocks)
        return [
            along(self.blocks[r], self.axis, [(i, (i + r) % count) for i in range(count)])
            for r in range(1, count)
        ]

    def take(self, got):
        self.slots = [self.blocks[0], *got]


class Once:
    def __init__(self, *sends):
        self.all = list(sends)

    def sends(self):
        return self.all

    def take(self, got):
        self.got = got


class Total:
    def __init__(self, value, axes):
        self.value = value
        self.rounds = [
            (axis, 1 << k) for axis in axes for k in range(lax.axis_size(axis).bit_length() - 1)
        ]

    def sends(self):
        if not self.rounds:
            return []
        axis, by = self.rounds.pop(0)
        return [along(self.value, axis, [(i, i ^ by) for i in range(lax.axis_size(axis))])]

    def take(self, got):
        for other in got:
            self.value = self.value + other


class Halving:
    def __init__(self, value, axes):
        bits = [
            (axis, k)
            for axis in axes
            for k in reversed(range(lax.axis_size(axis).bit_length() - 1))
        ]
        blocks = math.prod(lax.axis_size(axis) for axis in axes)
        rows, width = value.shape[0] // blocks, value.shape[1] // 2
        first = [bit for bit in bits if bit[0] != axes[0]]
        last = [bit for bit in bits if bit[0] == axes[0]]
        self.rounds = len(bits)
        self.groups = []
        for g, order in enumerate((first + last, first + last[::-1])):
            columns = value[:, g * width : (g + 1) * width]
            self.groups.append([columns.reshape((2,) * len(bits) + (rows, width)), list(bits), order])

    def sends(self):
        sent = []
        self.kept = []
        for value, left, order in self.groups:
            axis, k = bit = order.pop(0)
            dim = left.index(bit)
            left.pop(dim)
            mine = (lax.axis_index(axis) >> k) & 1
            pairs = [(i, i ^ (1 << k)) for i in range(lax.axis_size(axis))]
            self.kept.append(lax.dynamic_index_in_dim(value, mine, dim, keepdims=False))
            away = lax.dynamic_index_in_dim(value, 1 - mine, dim, keepdims=False)
            sent.append(along(away, axis, pairs))
        self.rounds -= 1
        return sent

    def take(self, got):
        for group, kept, other in zip(self.groups, self.kept, got):
            group[0] = (kept.astype(F32) + other.astype(F32)).astype(BF16)

    def total(self):
        return jnp.concatenate([group[0] for group in self.groups], axis=1)


def step(movers, work=None, *operands):
    sends = [mover.sends() for mover in movers]
    values = [[value for value, _ in group] for group in sends]
    values, operands = lax.optimization_barrier((values, operands))
    got = [
        [send(value) for value, (_, send) in zip(vals, group)] for vals, group in zip(values, sends)
    ]
    done = work(*operands) if work else ()
    got, done = lax.optimization_barrier((got, done))
    for mover, arrived in zip(movers, got):
        mover.take(arrived)
    return done


def slot_order(count):
    order = []
    for hop in range(1, count):
        order += [r for r in (hop, count - hop) if r not in order]
    return order + [0]


def after(value, *others):
    return lax.optimization_barrier((value, *others))[0]


def row_major(value):
    return with_layout_constraint(value, Layout(major_to_minor=tuple(range(value.ndim))))


def dot(left, right):
    return jnp.dot(left, right, preferred_element_type=F32)


def dot_nt(left, right):
    return lax.dot_general(left, right, (((1,), (1,)), ((), ())), preferred_element_type=F32)


def dot_tn(left, right):
    return lax.dot_general(left, right, (((0,), (0,)), ((), ())), preferred_element_type=F32)


def normalize(hidden):
    centred = hidden - jnp.mean(hidden, axis=-1, keepdims=True)
    variance = jnp.mean(centred * centred, axis=-1, keepdims=True)
    scale = lax.rsqrt(variance + LN_EPSILON)
    return centred * scale, scale


def norm_backward(grad, unit, scale, gain):
    scaled = grad * gain
    inner = jnp.mean(scaled * unit, axis=-1, keepdims=True)
    dhidden = scale * (scaled - jnp.mean(scaled, axis=-1, keepdims=True) - unit * inner)
    return dhidden, jnp.sum(grad * unit, axis=0), jnp.sum(grad, axis=0)


def gelu_tanh(values):
    return jax.nn.gelu(values, approximate=True)


def window_probs(q, keys, low_ref, high_ref, start):
    scores = dot_nt(keys, q) * (HEAD_DIM**-0.5)
    at = start + lax.broadcasted_iota(jnp.int32, scores.shape, 0)
    scores = jnp.where((at >= low_ref[...]) & (at <= high_ref[...]), scores, MASKED)
    expo = jnp.exp(scores - jnp.max(scores, axis=0, keepdims=True))
    return expo * (1.0 / jnp.sum(expo, axis=0, keepdims=True))


def attend_kernel(low_ref, high_ref, q_ref, k_ref, v_ref, o_ref):
    rows = q_ref.shape[0]
    span = rows + 2 * REACH
    start = pl.multiple_of(pl.program_id(1) * rows, rows)
    probs = window_probs(q_ref[...], k_ref[pl.ds(start, span), :], low_ref, high_ref, start)
    o_ref[...] = dot_tn(probs.astype(BF16), v_ref[pl.ds(start, span), :]).astype(BF16)


def attend_back_kernel(low_ref, high_ref, q_ref, k_ref, v_ref, g_ref, dq_ref, dk_ref, dv_ref):
    rows = q_ref.shape[0]
    span = rows + 2 * REACH
    start = pl.multiple_of(pl.program_id(1) * rows, rows)
    window = pl.ds(start, span)

    @pl.when(pl.program_id(1) == 0)
    def _():
        dk_ref[...] = jnp.zeros_like(dk_ref)
        dv_ref[...] = jnp.zeros_like(dv_ref)

    q, g, keys = q_ref[...], g_ref[...], k_ref[window, :]
    probs = window_probs(q, keys, low_ref, high_ref, start)
    dprobs = dot_nt(v_ref[window, :], g)
    offset = jnp.sum(dprobs * probs, axis=0, keepdims=True)
    dscores = (probs * (dprobs - offset) * (HEAD_DIM**-0.5)).astype(BF16)
    dv_ref[window, :] += dot(probs.astype(BF16), g)
    dk_ref[window, :] += dot(dscores, q)
    dq_ref[...] = dot_tn(dscores, keys).astype(BF16)


def attention_specs(rows, padded, heads):
    bounds = pl.BlockSpec((1, rows), lambda h, b: (0, b))
    queries = pl.BlockSpec((rows, HEAD_DIM), lambda h, b: (b, h))
    keys = pl.BlockSpec((padded, HEAD_DIM), lambda h, b: (0, h))
    values = pl.BlockSpec((padded, HEAD_DIM), lambda h, b: (0, h + heads))
    return bounds, queries, keys, values


def attend(low, high, qkv, padded_kv, heads):
    length, padded = qkv.shape[0], padded_kv.shape[0]
    rows = min(QUERY_ROWS, length)
    bounds, q_spec, k_spec, v_spec = attention_specs(rows, padded, heads)
    pairs = heads * length * (rows + 2 * REACH)
    return pl.pallas_call(
        attend_kernel,
        grid=(heads, length // rows),
        in_specs=[bounds, bounds, q_spec, k_spec, v_spec],
        out_specs=q_spec,
        out_shape=jax.ShapeDtypeStruct((length, heads * HEAD_DIM), BF16),
        cost_estimate=pl.CostEstimate(
            flops=16 * pairs * HEAD_DIM, transcendentals=pairs, bytes_accessed=8 << 20
        ),
        name="attend",
    )(low, high, qkv, padded_kv, padded_kv)


def attend_back(low, high, qkv, padded_kv, grads, heads):
    length, padded = qkv.shape[0], padded_kv.shape[0]
    rows = min(QUERY_ROWS, length)
    bounds, q_spec, k_spec, v_spec = attention_specs(rows, padded, heads)
    pairs = heads * length * (rows + 2 * REACH)
    total = jax.ShapeDtypeStruct((padded, heads * HEAD_DIM), F32)
    return pl.pallas_call(
        attend_back_kernel,
        grid=(heads, length // rows),
        in_specs=[bounds, bounds, q_spec, k_spec, v_spec, q_spec],
        out_specs=(q_spec, k_spec, k_spec),
        out_shape=(jax.ShapeDtypeStruct((length, heads * HEAD_DIM), BF16), total, total),
        cost_estimate=pl.CostEstimate(
            flops=32 * pairs * HEAD_DIM, transcendentals=pairs, bytes_accessed=20 << 20
        ),
        name="attend_back",
    )(low, high, qkv, padded_kv, padded_kv, grads)


def place_kernel(sizes, me_ref, *refs):
    at = 0
    for r, size in enumerate(sizes):
        terms = refs[at : at + size]
        at += size

        @pl.when(pl.program_id(0) == r)
        def _(terms=terms):
            value = terms[0][...]
            for term in terms[1:]:
                value = value + term[...]
            refs[-1][...] = value.astype(refs[-1].dtype)


def placed(slots, dtype, me):
    count = len(slots)
    share, width = slots[0][0].shape
    flat = [term for slot in slots for term in slot]
    whole = pl.BlockSpec((share, width), lambda r, me_ref: (0, 0))
    return pl.pallas_call(
        functools.partial(place_kernel, [len(slot) for slot in slots]),
        grid_spec=pltpu.PrefetchScalarGridSpec(
            num_scalar_prefetch=1,
            grid=(count,),
            in_specs=[whole] * len(flat),
            out_specs=pl.BlockSpec(
                (share, width), lambda r, me_ref: (lax.rem(me_ref[0] - r + count, count), 0)
            ),
        ),
        out_shape=jax.ShapeDtypeStruct((count * share, width), dtype),
        cost_estimate=pl.CostEstimate(
            flops=0, transcendentals=0, bytes_accessed=6 * count * share * width
        ),
        name="place",
    )(me.reshape(1), *flat)


def halves(value):
    top = value.astype(BF16)
    return top, (value - top.astype(F32)).astype(BF16)


def newton_schulz_kernel(steps, in_ref, out_ref, top, rest, iterate=None):
    opening = iterate is None
    iterate = out_ref if opening else iterate
    depth = top.shape[1]
    chunk = min(1024, depth)
    chunks = depth // chunk

    def columns(c):
        return pl.ds(pl.multiple_of(c * chunk, chunk), chunk)

    def load(c, total):
        part = in_ref[columns(c), :].astype(F32)
        iterate[:, columns(c)] = part.T
        return total + jnp.sum(part * part, axis=(0, 1), keepdims=True)

    if opening:
        norm = jnp.sqrt(lax.fori_loop(0, chunks, load, jnp.zeros((1, 1), F32)))
        inverse = 1.0 / (norm + 1e-07)

    def split(c, carry):
        value = iterate[:, columns(c)] * inverse if opening else in_ref[:, columns(c)]
        iterate[:, columns(c)] = value
        top[:, columns(c)], rest[:, columns(c)] = halves(value)
        return carry

    lax.fori_loop(0, chunks, split, 0)

    def step(index, carry):
        cross = dot_nt(rest[...], top[...])
        gram = dot_nt(top[...], top[...]) + (cross + cross.T)
        gram_top, gram_rest = halves(gram)
        cross = dot(gram_top, gram_rest)
        square = dot(gram_top, gram_top) + (cross + cross.T)
        poly_top, poly_rest = halves(NS_COEFFS[1] * gram + NS_COEFFS[2] * square)

        def update(c, carry):
            here = columns(c)
            change = dot(poly_top, top[:, here]) + dot(poly_rest, top[:, here])
            value = NS_COEFFS[0] * iterate[:, here] + (change + dot(poly_top, rest[:, here]))
            iterate[:, here] = value
            top[:, here], rest[:, here] = halves(value)
            return carry

        return lax.fori_loop(0, chunks, update, carry)

    lax.fori_loop(0, steps, step, 0)

    def store(c, carry):
        out_ref[columns(c), :] = iterate[:, columns(c)].T.astype(BF16)
        return carry

    if not opening:
        lax.fori_loop(0, chunks, store, 0)


def newton_schulz_part(steps, value, out, depth, width, scratch):
    return pl.pallas_call(
        functools.partial(newton_schulz_kernel, steps),
        out_shape=out,
        in_specs=[pl.BlockSpec(memory_space=pltpu.VMEM)],
        out_specs=pl.BlockSpec(memory_space=pltpu.VMEM),
        scratch_shapes=[pltpu.VMEM((width, depth), BF16), pltpu.VMEM((width, depth), BF16), *scratch],
        cost_estimate=pl.CostEstimate(
            flops=2 * steps * width * width * (5 * depth + 2 * width),
            transcendentals=0,
            bytes_accessed=6 * depth * width,
        ),
        name="newton_schulz",
    )(value)


def orthogonal_start(owned):
    depth, width = owned.shape[0] * owned.shape[1], owned.shape[2]
    out = jax.ShapeDtypeStruct((width, depth), F32)
    return newton_schulz_part(NS_STEPS // 2, owned.reshape(depth, width), out, depth, width, [])


def orthogonal_end(iterate, group):
    width, depth = iterate.shape
    out = jax.ShapeDtypeStruct((depth, width), BF16)
    scratch = [pltpu.VMEM((width, depth), F32)]
    done = newton_schulz_part(NS_STEPS - NS_STEPS // 2, iterate, out, depth, width, scratch)
    return done.reshape(group, depth // group, width)


def to_owners(blocks):
    copies = lax.axis_size("shard") * lax.axis_size("ctx") // len(blocks)
    return jnp.stack([block.astype(BF16) for block in blocks for _ in range(copies)])


def swapped(value):
    return value, functools.partial(
        lax.all_to_all, axis_name=WEIGHT_AXES, split_axis=0, concat_axis=0, tiled=True
    )


def from_owners(back, count):
    copies = back.shape[0] // count
    return [back[b * copies].astype(F32) for b in range(count)]


def column_blocks(value):
    return [value[:, at : at + BW] for at in range(0, value.shape[1], BW)]


def gather_rows(value):
    return lax.all_gather(value, WEIGHT_AXES, axis=0, tiled=True)


def scatter_rows(value):
    return lax.psum_scatter(value, WEIGHT_AXES, scatter_dimension=0, tiled=True)


def blend(old, grad):
    return BETA * old + (1.0 - BETA) * grad


def body(
    hidden_in,
    doc_span,
    cotangent,
    w_query,
    w_key,
    w_value,
    w_out,
    w_inner,
    w_outer,
    norm_gains,
    norm_biases,
    mom_query,
    mom_key,
    mom_value,
    mom_out,
    mom_inner,
    mom_outer,
    gain_moment,
    bias_moment,
):
    tp = lax.axis_size("tp")
    me = lax.axis_index("tp")
    hidden = hidden_in[0]
    length, width = hidden.shape
    share = length // tp
    local = w_query.shape[1]
    heads = local // HEAD_DIM

    def slice_of(value, r):
        return lax.dynamic_slice_in_dim(value, lax.rem(me - r + tp, tp) * share, share, 0)

    full_qkv = gather_rows(jnp.concatenate([w_query, w_key, w_value], axis=1).astype(BF16))
    w_out_t = Gather(w_out.T.astype(BF16), "tp")
    for _ in range(tp - 1):
        step([w_out_t])
    full_out_t = gather_rows(jnp.concatenate(w_out_t.slots(), axis=1))
    full_inner = gather_rows(w_inner.astype(BF16))
    full_outer_t = gather_rows(w_outer.T.astype(BF16))

    qkv = dot(hidden, full_qkv).astype(BF16)
    own_kv = qkv[:, local:]
    ctx = lax.axis_size("ctx")
    edges = Once(
        along(own_kv[length - REACH :], "ctx", upward(0, ctx - 1)),
        along(own_kv[:REACH], "ctx", downward(1, ctx)),
    )
    step([edges])
    padded_kv = jnp.concatenate([edges.got[0], own_kv, edges.got[1]], axis=0)

    position = jnp.arange(length, dtype=jnp.int32)
    anchor = lax.axis_index("ctx") * length - REACH
    low = jnp.maximum(doc_span[0] - anchor, position[None])
    high = jnp.minimum(doc_span[1] - anchor, position[None] + 2 * REACH)
    attended = attend(low, high, qkv, padded_kv, heads)

    all_heads = Gather(attended, "tp")
    mom_outer_t, mom_out_t = step([all_heads], lambda a, b: (a.T, b.T), mom_outer, mom_out)
    for _ in range(tp - 2):
        step([all_heads])
    head_slots = all_heads.slots()

    order = slot_order(tp)
    first, rest = order[:2], order[2:]
    normed_slots, pre_slots, act_slots, parts = ([None] * tp for _ in range(4))
    own = []

    def forward(slots, *head_slots):
        made = []
        for r in slots:
            attended_r = jnp.concatenate([slice_of(slot, r) for slot in head_slots], axis=1)
            branch = dot_nt(attended_r, full_out_t)
            unit, scale = normalize(slice_of(hidden, r).astype(F32) + branch)
            normed = unit * norm_gains[0] + norm_biases[0]
            normed_low = normed.astype(BF16)
            pre = dot(normed_low, full_inner)
            act = gelu_tanh(pre).astype(BF16)
            part = dot_nt(act, full_outer_t)
            made.append((normed_low, pre, act, part if r == 0 else part.astype(BF16)))
            if r == 0:
                made.append((unit, scale, normed))
        return made

    def keep(slots, made):
        for r, values in zip(slots, made):
            normed_slots[r], pre_slots[r], act_slots[r], parts[r] = values

    keep(first, forward(first, *head_slots))
    ffn_sum = Scatter(parts, "tp")
    made = step([ffn_sum], functools.partial(forward, rest), *head_slots)
    unit_one, scale_one, own_normed = made[-1]
    keep(rest, made)

    def slopes_of(*pres):
        return [jax.vjp(gelu_tanh, pre)[1](jnp.ones_like(pre))[0] for pre in pres]

    slopes = [None] * tp
    half = tp // 2
    slopes[:half] = step([ffn_sum], slopes_of, *pre_slots[:half])
    slopes[half:] = step([ffn_sum], slopes_of, *pre_slots[half:])
    for _ in range(tp - 4):
        step([ffn_sum])

    unit_two, scale_two = normalize(own_normed + ffn_sum.total())
    own_out = (unit_two * norm_gains[1] + norm_biases[1]).astype(BF16)
    seed = slice_of(cotangent[0], 0).astype(F32)
    grad_two, gain_two, shift_two = norm_backward(seed, unit_two, scale_two, norm_gains[1])
    dffn_all = Gather(grad_two.astype(BF16), "tp")
    dpre_slots, parts = [None] * tp, [None] * tp

    def backward(*pairs):
        made = []
        for dffn, slope in pairs:
            dpre = (dot(dffn, full_outer_t) * slope).astype(BF16)
            made.append((dpre, dot_nt(dpre, full_inner).astype(BF16)))
        return made

    def keep_back(slots, made):
        for r, values in zip(slots, made):
            dpre_slots[r], parts[r] = values

    step([dffn_all])
    keep_back([0], step([dffn_all], backward, (dffn_all.slot(0), slopes[0])))
    middle = [r for r in rest if r]
    ready = [(dffn_all.slot(r), slopes[r]) for r in middle] if tp == 4 else []
    made = step([dffn_all], backward, *ready)
    for _ in range(tp - 4):
        step([dffn_all])
    if not ready:
        made = backward(*[(dffn_all.slot(r), slopes[r]) for r in middle])
    keep_back(middle, made)
    dffn_slots = dffn_all.slots()
    out_all = Gather(own_out, "tp")
    keep_back(first, step([out_all], backward, *[(dffn_slots[r], slopes[r]) for r in first]))

    dnormed_sum = Scatter(parts, "tp")

    def weight_grad(lefts, rights):
        return dot_tn(jnp.concatenate(lefts, axis=0), jnp.concatenate(rights, axis=0)).astype(BF16)

    grad_outer_t = step([out_all, dnormed_sum], weight_grad, dffn_slots, act_slots)
    grad_outer_t = scatter_rows(grad_outer_t)
    grad_inner = step([out_all, dnormed_sum], weight_grad, normed_slots, dpre_slots)
    grad_inner = scatter_rows(grad_inner)
    layer_out = step([dnormed_sum], lambda *slots: placed(slots, BF16, me), *out_all.terms())[None]
    for _ in range(tp - 4):
        step([dnormed_sum])
    dnormed = grad_two + dnormed_sum.total()

    grad_one, gain_one, shift_one = norm_backward(dnormed, unit_one, scale_one, norm_gains[0])
    dbranch_low = grad_one.astype(BF16)
    dattended_all = dot(dbranch_low, full_out_t).astype(BF16)
    blocks = [dattended_all[:, (-r % tp) * local : (-r % tp + 1) * local] for r in range(tp)]
    dattended = Exchange(blocks, "tp")
    totals = Total(
        jnp.stack([gain_one, gain_two, shift_one, shift_two]), ("ctx", "shard", "tp")
    )
    step([dattended])
    part = width // tp
    dbranch = Exchange(
        [
            lax.dynamic_slice_in_dim(dbranch_low, lax.rem(me + r, tp) * part, part, 1)
            for r in range(tp)
        ],
        "tp",
    )

    def attention_back(*slots):
        return attend_back(low, high, qkv, padded_kv, placed([[slot] for slot in slots], BF16, me), heads)

    dq_low, key_grad, value_grad = step([dbranch, totals], attention_back, *dattended.slots)

    def kv_rows(start, count):
        rows = slice(start, start + count)
        return jnp.concatenate([key_grad[rows], value_grad[rows]], axis=1)

    edges = Once(
        along(kv_rows(0, REACH).astype(BF16), "ctx", downward(1, ctx)),
        along(kv_rows(length + REACH, REACH).astype(BF16), "ctx", upward(0, ctx - 1)),
    )
    rows = w_query.shape[0]
    group = width // rows

    def out_pieces(dbranch_slots, head_slots):
        columns = placed([[slot] for slot in dbranch_slots], BF16, me)
        sums = [dot_tn(columns, slot).astype(BF16).reshape(-1, rows, local) for slot in head_slots]
        return row_major(jnp.stack(sums, axis=1).reshape(group * rows, local))

    step([edges])
    from_above, from_below = (edge.astype(F32) for edge in edges.got)
    beyond = length - REACH
    added = jnp.pad(from_above, ((beyond, 0), (0, 0))) + jnp.pad(from_below, ((0, beyond), (0, 0)))
    dqkv = jnp.concatenate([dq_low, (kv_rows(REACH, length) + added).astype(BF16)], axis=1)
    grad_qkv = row_major(dot_tn(hidden, dqkv).astype(BF16))
    qkv_sum = Halving(grad_qkv, WEIGHT_AXES)

    parts = [None] * tp

    def input_terms(slots, dqkv):
        rows = jnp.concatenate([slice_of(dqkv, r) for r in slots], axis=0)
        sums = dot_nt(rows, full_qkv).astype(BF16)
        return [sums[n * share : (n + 1) * share] for n in range(len(slots))]

    for r, value in zip(first, step([qkv_sum], functools.partial(input_terms, first), dqkv)):
        parts[r] = value
    input_sum = Scatter(parts, "tp")

    def between(dqkv, dbranch_slots, head_slots, grad_inner, grad_outer_t):
        pieces = out_pieces(dbranch_slots, head_slots)
        moments = blend(mom_inner, grad_inner), blend(mom_outer_t, grad_outer_t)
        blocks = to_owners(sum(map(column_blocks, moments), []))
        return input_terms(rest, dqkv), moments, blocks, pieces

    terms, (moment_inner, moment_outer_t), blocks, pieces = step(
        [input_sum, qkv_sum, totals],
        between,
        dqkv,
        dbranch.slots,
        head_slots,
        grad_inner,
        grad_outer_t,
    )
    grad_inner, grad_outer_t = grad_inner.astype(F32), grad_outer_t.astype(F32)
    for r, value in zip(rest, terms):
        parts[r] = value
    grad_piece = scatter_rows(pieces)
    owners = Once(swapped(blocks))
    step([input_sum, qkv_sum, totals, owners])
    homes = [
        (p * tp + t, (t * (group // tp) + p // tp) * tp + (t - p % tp) % tp)
        for p in range(group)
        for t in range(tp)
    ]
    piece = Once(along(grad_piece, (*WEIGHT_AXES, "tp"), homes))
    iterate = step([input_sum, totals, piece], orthogonal_start, owners.got[0])
    for _ in range(tp - 4):
        step([input_sum])
    while qkv_sum.rounds:
        step([qkv_sum])
    own_input = Gather((grad_one + input_sum.total()).astype(BF16), "tp")

    grad_query, grad_key, grad_value = jnp.split(qkv_sum.total().astype(F32), 3, axis=1)
    grad_out_t = row_major(piece.got[0]).astype(F32)
    moment_query = blend(mom_query, grad_query)
    moment_key = blend(mom_key, grad_key)
    moment_value = blend(mom_value, grad_value)
    moment_out_t = blend(mom_out_t, grad_out_t)
    moments = moment_query, moment_key, moment_value, moment_out_t
    shard = lax.axis_size("shard")
    at_shard = lax.axis_index("shard")
    blocks = [row_major(m.astype(BF16)) for m in sum(map(column_blocks, moments), [])]
    blocks = row_major(jnp.stack(blocks))
    blocks = blocks.reshape(shard, -1, *blocks.shape[1:])

    def turned(value, r):
        return lax.dynamic_index_in_dim(value, lax.rem(at_shard + r, shard), 0, keepdims=False)

    owners = Exchange([turned(blocks, r) for r in range(shard)], "shard")
    finish = functools.partial(orthogonal_end, group=group)
    done = step([own_input, owners, totals], finish, iterate)
    spread = [owners.slots]
    for by in range(1, ctx):
        pairs = [(i, (i + by) % ctx) for i in range(ctx)]
        peers = Once(*[along(slot, "ctx", pairs) for slot in owners.slots])
        step([peers])
        spread.append(peers.got)
    at_ctx = lax.axis_index("ctx")
    owned = jnp.zeros((shard, ctx, *blocks.shape[2:]), BF16)
    for by, slots in enumerate(spread):
        for r, slot in enumerate(slots):
            where = lax.rem(at_shard - r + shard, shard), lax.rem(at_ctx - by + ctx, ctx)
            owned = lax.dynamic_update_slice(owned, slot[None], (*where, 0, 0))

    def update_ffn(back):
        ortho = from_owners(back, 2 * moment_inner.shape[1] // BW)
        half = len(ortho) // 2
        return (
            w_inner - MATRIX_RATE * jnp.concatenate(ortho[:half], axis=1),
            w_outer - MATRIX_RATE * jnp.concatenate(ortho[half:], axis=1).T,
        )

    ortho = Once(swapped(done))
    iterate = step([own_input, ortho], orthogonal_start, owned.reshape(group, rows, BW))
    done = step([own_input], finish, iterate).reshape(shard, ctx, rows, BW)
    for _ in range(tp - 4):
        step([own_input])
    done = lax.dynamic_index_in_dim(done, at_ctx, 1, keepdims=False)
    attn = Exchange([turned(done, r) for r in range(shard)], "shard")

    def closing(back, *slots):
        return update_ffn(back), placed(slots, F32, me)

    (new_inner, new_outer), input_grad = step([attn], closing, ortho.got[0], *own_input.terms())
    input_grad = input_grad[None]
    ortho = jnp.stack(attn.slots)
    ortho = [
        lax.dynamic_index_in_dim(ortho, lax.rem(at_shard - b + shard, shard), 0, keepdims=False)
        for b in range(shard)
    ]
    ortho = [block.astype(F32) for block in ortho]
    while totals.rounds:
        step([totals])
    gain_grad, bias_grad = totals.value[:2], totals.value[2:]
    new_query = w_query - MATRIX_RATE * ortho[0]
    new_key = w_key - MATRIX_RATE * ortho[1]
    new_value = w_value - MATRIX_RATE * ortho[2]
    new_out = w_out - MATRIX_RATE * ortho[3].T

    tokens_all = length * lax.axis_size("shard") * ctx
    gain_moment_new = blend(gain_moment, gain_grad)
    bias_moment_new = blend(bias_moment, bias_grad)
    new_gains = norm_gains - VECTOR_RATE * gain_moment_new / math.sqrt(tokens_all)
    new_biases = norm_biases - VECTOR_RATE * bias_moment_new / math.sqrt(tokens_all)
    return (
        layer_out,
        input_grad,
        grad_query,
        grad_key,
        grad_value,
        grad_out_t.T,
        grad_inner,
        grad_outer_t.T,
        gain_grad,
        bias_grad,
        moment_query,
        moment_key,
        moment_value,
        moment_out_t.T,
        moment_inner,
        moment_outer_t.T,
        gain_moment_new,
        bias_moment_new,
        new_query,
        new_key,
        new_value,
        new_out,
        new_inner,
        new_outer,
        new_gains,
        new_biases,
    )


def solution(mesh):
    tokens = P("shard", "ctx", None)
    by_rows = P(WEIGHT_AXES, "tp")
    by_columns = P("tp", WEIGHT_AXES)
    matrices = (by_rows, by_rows, by_rows, by_columns, by_rows, by_columns)
    return jax.shard_map(
        body,
        mesh=mesh,
        in_specs=(tokens, P(None, "shard", "ctx"), tokens, *matrices, P(), P(), *matrices, P(), P()),
        out_specs=(tokens, tokens, *matrices, P(), P(), *matrices, P(), P(), *matrices, P(), P()),
        check_vma=False,
    )
```

```python
import functools
import math

import jax
import jax.numpy as jnp
from jax import lax
from jax.experimental import pallas as pl
from jax.experimental.layout import Layout, with_layout_constraint
from jax.experimental.pallas import tpu as pltpu
from jax.sharding import PartitionSpec as P

HEAD_DIM = 128
REACH = 512
BW = 512
NS_STEPS = 5
QUERY_ROWS = 256

NS_COEFFS = (3.4445, -4.775, 2.0315)
LN_EPSILON = 1e-12
BETA = 0.5
MATRIX_RATE = 0.5
VECTOR_RATE = 0.3
MASKED = -1e30
WEIGHT_AXES = ("shard", "ctx")
BF16 = jnp.bfloat16
F32 = jnp.float32


def along(value, axis, pairs):
    return value, functools.partial(lax.ppermute, axis_name=axis, perm=pairs)


def upward(first, last):
    return [(i, i + 1) for i in range(first, last)]


def downward(first, last):
    return [(i, i - 1) for i in range(first, last)]


class Gather:
    def __init__(self, block, axis):
        self.count, self.axis = lax.axis_size(axis), axis
        self.block, self.ups, self.downs = block, [], []

    def sends(self):
        step = len(self.ups) + 1
        up, down = (self.ups[-1], self.downs[-1]) if self.ups else (self.block, self.block)
        return [
            along(up, self.axis, upward(step - 1, self.count - 1)),
            along(down, self.axis, downward(1, self.count - step + 1)),
        ]

    def take(self, got):
        self.ups.append(got[0])
        self.downs.append(got[1])

    def slot(self, r):
        return self.ups[r - 1] + self.downs[self.count - r - 1] if r else self.block

    def slots(self):
        return [self.slot(r) for r in range(self.count)]

    def terms(self):
        pairs = [[self.ups[r - 1], self.downs[self.count - r - 1]] for r in range(1, self.count)]
        return [[self.block], *pairs]


class Scatter:
    def __init__(self, parts, axis):
        self.count, self.axis = lax.axis_size(axis), axis
        self.parts, self.step, self.got = parts, 0, None

    def sends(self):
        self.step += 1
        step, count = self.step, self.count
        terms = [self.parts[step], self.parts[count - step]]
        if self.got:
            terms = [
                term.astype(F32) + got.astype(F32) for term, got in zip(terms, self.got)
            ]
        return [
            along(terms[0].astype(BF16), self.axis, upward(0, step)),
            along(terms[1].astype(BF16), self.axis, downward(count - step, count)),
        ]

    def take(self, got):
        self.got = got

    def total(self):
        return self.parts[0].astype(F32) + (self.got[0].astype(F32) + self.got[1].astype(F32))


class Exchange:
    def __init__(self, blocks, axis):
        self.blocks, self.axis = blocks, axis

    def sends(self):
        count = len(self.blocks)
        return [
            along(self.blocks[r], self.axis, [(i, (i + r) % count) for i in range(count)])
            for r in range(1, count)
        ]

    def take(self, got):
        self.slots = [self.blocks[0], *got]


class Once:
    def __init__(self, *sends):
        self.all = list(sends)

    def sends(self):
        return self.all

    def take(self, got):
        self.got = got


def step(movers, work=None, *operands):
    sends = [mover.sends() for mover in movers]
    values = [[value for value, _ in group] for group in sends]
    values, operands = lax.optimization_barrier((values, operands))
    got = [
        [send(value) for value, (_, send) in zip(vals, group)] for vals, group in zip(values, sends)
    ]
    done = work(*operands) if work else ()
    got, done = lax.optimization_barrier((got, done))
    for mover, arrived in zip(movers, got):
        mover.take(arrived)
    return done


def slot_order(count):
    order = []
    for hop in range(1, count):
        order += [r for r in dict.fromkeys((hop, count - hop)) if r not in order]
    return order + [0]


def after(value, *others):
    return lax.optimization_barrier((value, *others))[0]


def row_major(value):
    return with_layout_constraint(value, Layout(major_to_minor=tuple(range(value.ndim))))


def dot(left, right):
    return jnp.dot(left, right, preferred_element_type=F32)


def dot_nt(left, right):
    return lax.dot_general(left, right, (((1,), (1,)), ((), ())), preferred_element_type=F32)


def dot_tn(left, right):
    return lax.dot_general(left, right, (((0,), (0,)), ((), ())), preferred_element_type=F32)


def normalize(hidden):
    centred = hidden - jnp.mean(hidden, axis=-1, keepdims=True)
    variance = jnp.mean(centred * centred, axis=-1, keepdims=True)
    scale = lax.rsqrt(variance + LN_EPSILON)
    return centred * scale, scale


def norm_backward(grad, unit, scale, gain):
    scaled = grad * gain
    inner = jnp.mean(scaled * unit, axis=-1, keepdims=True)
    dhidden = scale * (scaled - jnp.mean(scaled, axis=-1, keepdims=True) - unit * inner)
    return dhidden, jnp.sum(grad * unit, axis=0), jnp.sum(grad, axis=0)


def gelu_tanh(values):
    return jax.nn.gelu(values, approximate=True)


def window_probs(q, keys, low_ref, high_ref, start):
    scores = dot_nt(keys, q) * (HEAD_DIM**-0.5)
    at = start + lax.broadcasted_iota(jnp.int32, scores.shape, 0)
    scores = jnp.where((at >= low_ref[...]) & (at <= high_ref[...]), scores, MASKED)
    expo = jnp.exp(scores - jnp.max(scores, axis=0, keepdims=True))
    return expo * (1.0 / jnp.sum(expo, axis=0, keepdims=True))


def attend_kernel(low_ref, high_ref, q_ref, k_ref, v_ref, o_ref):
    rows = q_ref.shape[0]
    span = rows + 2 * REACH
    start = pl.multiple_of(pl.program_id(1) * rows, rows)
    probs = window_probs(q_ref[...], k_ref[pl.ds(start, span), :], low_ref, high_ref, start)
    o_ref[...] = dot_tn(probs.astype(BF16), v_ref[pl.ds(start, span), :]).astype(BF16)


def attend_back_kernel(low_ref, high_ref, q_ref, k_ref, v_ref, g_ref, dq_ref, dk_ref, dv_ref):
    rows = q_ref.shape[0]
    span = rows + 2 * REACH
    start = pl.multiple_of(pl.program_id(1) * rows, rows)
    window = pl.ds(start, span)

    @pl.when(pl.program_id(1) == 0)
    def _():
        dk_ref[...] = jnp.zeros_like(dk_ref)
        dv_ref[...] = jnp.zeros_like(dv_ref)

    q, g, keys = q_ref[...], g_ref[...], k_ref[window, :]
    probs = window_probs(q, keys, low_ref, high_ref, start)
    dprobs = dot_nt(v_ref[window, :], g)
    offset = jnp.sum(dprobs * probs, axis=0, keepdims=True)
    dscores = (probs * (dprobs - offset) * (HEAD_DIM**-0.5)).astype(BF16)
    dv_ref[window, :] += dot(probs.astype(BF16), g)
    dk_ref[window, :] += dot(dscores, q)
    dq_ref[...] = dot_tn(dscores, keys).astype(BF16)


def attention_specs(rows, padded, heads):
    bounds = pl.BlockSpec((1, rows), lambda h, b: (0, b))
    queries = pl.BlockSpec((rows, HEAD_DIM), lambda h, b: (b, h))
    keys = pl.BlockSpec((padded, HEAD_DIM), lambda h, b: (0, h))
    values = pl.BlockSpec((padded, HEAD_DIM), lambda h, b: (0, h + heads))
    return bounds, queries, keys, values


def attend(low, high, qkv, padded_kv, heads):
    length, padded = qkv.shape[0], padded_kv.shape[0]
    rows = min(QUERY_ROWS, length)
    bounds, q_spec, k_spec, v_spec = attention_specs(rows, padded, heads)
    pairs = heads * length * (rows + 2 * REACH)
    return pl.pallas_call(
        attend_kernel,
        grid=(heads, length // rows),
        in_specs=[bounds, bounds, q_spec, k_spec, v_spec],
        out_specs=q_spec,
        out_shape=jax.ShapeDtypeStruct((length, heads * HEAD_DIM), BF16),
        cost_estimate=pl.CostEstimate(
            flops=16 * pairs * HEAD_DIM, transcendentals=pairs, bytes_accessed=8 << 20
        ),
        name="attend",
    )(low, high, qkv, padded_kv, padded_kv)


def attend_back(low, high, qkv, padded_kv, grads, heads):
    length, padded = qkv.shape[0], padded_kv.shape[0]
    rows = min(QUERY_ROWS, length)
    bounds, q_spec, k_spec, v_spec = attention_specs(rows, padded, heads)
    pairs = heads * length * (rows + 2 * REACH)
    total = jax.ShapeDtypeStruct((padded, heads * HEAD_DIM), F32)
    return pl.pallas_call(
        attend_back_kernel,
        grid=(heads, length // rows),
        in_specs=[bounds, bounds, q_spec, k_spec, v_spec, q_spec],
        out_specs=(q_spec, k_spec, k_spec),
        out_shape=(jax.ShapeDtypeStruct((length, heads * HEAD_DIM), BF16), total, total),
        cost_estimate=pl.CostEstimate(
            flops=32 * pairs * HEAD_DIM, transcendentals=pairs, bytes_accessed=20 << 20
        ),
        name="attend_back",
    )(low, high, qkv, padded_kv, padded_kv, grads)


def place_kernel(sizes, me_ref, *refs):
    at = 0
    for r, size in enumerate(sizes):
        terms = refs[at : at + size]
        at += size

        @pl.when(pl.program_id(0) == r)
        def _(terms=terms):
            value = terms[0][...]
            for term in terms[1:]:
                value = value + term[...]
            refs[-1][...] = value.astype(refs[-1].dtype)


def placed(slots, dtype, me):
    count = len(slots)
    share, width = slots[0][0].shape
    flat = [term for slot in slots for term in slot]
    whole = pl.BlockSpec((share, width), lambda r, me_ref: (0, 0))
    return pl.pallas_call(
        functools.partial(place_kernel, [len(slot) for slot in slots]),
        grid_spec=pltpu.PrefetchScalarGridSpec(
            num_scalar_prefetch=1,
            grid=(count,),
            in_specs=[whole] * len(flat),
            out_specs=pl.BlockSpec(
                (share, width), lambda r, me_ref: (lax.rem(me_ref[0] - r + count, count), 0)
            ),
        ),
        out_shape=jax.ShapeDtypeStruct((count * share, width), dtype),
        cost_estimate=pl.CostEstimate(
            flops=0, transcendentals=0, bytes_accessed=6 * count * share * width
        ),
        name="place",
    )(me.reshape(1), *flat)


def halves(value):
    top = value.astype(BF16)
    return top, (value - top.astype(F32)).astype(BF16)


def newton_schulz_kernel(steps, in_ref, out_ref, top, rest, iterate=None):
    opening = iterate is None
    iterate = out_ref if opening else iterate
    depth = top.shape[1]
    chunk = min(1024, depth)
    chunks = depth // chunk

    def columns(c):
        return pl.ds(pl.multiple_of(c * chunk, chunk), chunk)

    def load(c, total):
        part = in_ref[columns(c), :].astype(F32)
        iterate[:, columns(c)] = part.T
        return total + jnp.sum(part * part, axis=(0, 1), keepdims=True)

    if opening:
        norm = jnp.sqrt(lax.fori_loop(0, chunks, load, jnp.zeros((1, 1), F32)))
        inverse = 1.0 / (norm + 1e-07)

    def split(c, carry):
        value = iterate[:, columns(c)] * inverse if opening else in_ref[:, columns(c)]
        iterate[:, columns(c)] = value
        top[:, columns(c)], rest[:, columns(c)] = halves(value)
        return carry

    lax.fori_loop(0, chunks, split, 0)

    def step(index, carry):
        gram = dot_nt(top[...], top[...])
        gram_top, gram_rest = halves(gram)
        cross = dot(gram_top, gram_rest)
        square = dot(gram_top, gram_top) + (cross + cross.T)
        poly_top, poly_rest = halves(NS_COEFFS[1] * gram + NS_COEFFS[2] * square)

        def update(c, carry):
            here = columns(c)
            change = dot(poly_top, top[:, here]) + dot(poly_rest, top[:, here])
            value = NS_COEFFS[0] * iterate[:, here] + (change + dot(poly_top, rest[:, here]))
            iterate[:, here] = value
            top[:, here], rest[:, here] = halves(value)
            return carry

        return lax.fori_loop(0, chunks, update, carry)

    lax.fori_loop(0, steps, step, 0)

    def store(c, carry):
        out_ref[columns(c), :] = iterate[:, columns(c)].T.astype(BF16)
        return carry

    if not opening:
        lax.fori_loop(0, chunks, store, 0)


def newton_schulz_part(steps, value, out, depth, width, scratch):
    return pl.pallas_call(
        functools.partial(newton_schulz_kernel, steps),
        out_shape=out,
        in_specs=[pl.BlockSpec(memory_space=pltpu.VMEM)],
        out_specs=pl.BlockSpec(memory_space=pltpu.VMEM),
        scratch_shapes=[pltpu.VMEM((width, depth), BF16), pltpu.VMEM((width, depth), BF16), *scratch],
        cost_estimate=pl.CostEstimate(
            flops=2 * steps * width * width * (4 * depth + 2 * width),
            transcendentals=0,
            bytes_accessed=6 * depth * width,
        ),
        name="newton_schulz",
    )(value)


def orthogonal_start(owned):
    depth, width = owned.shape[0] * owned.shape[1], owned.shape[2]
    out = jax.ShapeDtypeStruct((width, depth), F32)
    return newton_schulz_part(NS_STEPS // 2, owned.reshape(depth, width), out, depth, width, [])


def orthogonal_end(iterate, group):
    width, depth = iterate.shape
    out = jax.ShapeDtypeStruct((depth, width), BF16)
    scratch = [pltpu.VMEM((width, depth), F32)]
    done = newton_schulz_part(NS_STEPS - NS_STEPS // 2, iterate, out, depth, width, scratch)
    return done.reshape(group, depth // group, width)


def to_owners(blocks):
    copies = lax.axis_size("shard") * lax.axis_size("ctx") // len(blocks)
    return jnp.stack([block.astype(BF16) for block in blocks for _ in range(copies)])


def swapped(value):
    return value, functools.partial(
        lax.all_to_all, axis_name=WEIGHT_AXES, split_axis=0, concat_axis=0, tiled=True
    )


def from_owners(back, count):
    copies = back.shape[0] // count
    return [back[b * copies].astype(F32) for b in range(count)]


def column_blocks(value):
    return [value[:, at : at + BW] for at in range(0, value.shape[1], BW)]


def gather_rows(value):
    return lax.all_gather(value, WEIGHT_AXES, axis=0, tiled=True)


def scatter_rows(value):
    return lax.psum_scatter(value, WEIGHT_AXES, scatter_dimension=0, tiled=True)


def blend(old, grad):
    return BETA * old + (1.0 - BETA) * grad


def body(
    hidden_in,
    doc_span,
    cotangent,
    w_query,
    w_key,
    w_value,
    w_out,
    w_inner,
    w_outer,
    norm_gains,
    norm_biases,
    mom_query,
    mom_key,
    mom_value,
    mom_out,
    mom_inner,
    mom_outer,
    gain_moment,
    bias_moment,
):
    tp = lax.axis_size("tp")
    me = lax.axis_index("tp")
    hidden = hidden_in[0]
    length, width = hidden.shape
    share = length // tp
    local = w_query.shape[1]
    heads = local // HEAD_DIM

    def slice_of(value, r):
        return lax.dynamic_slice_in_dim(value, lax.rem(me - r + tp, tp) * share, share, 0)

    full_qkv = gather_rows(jnp.concatenate([w_query, w_key, w_value], axis=1).astype(BF16))
    w_out_t = Gather(w_out.T.astype(BF16), "tp")
    for _ in range(tp - 1):
        step([w_out_t])
    full_out_t = gather_rows(jnp.concatenate(w_out_t.slots(), axis=1))
    full_inner = gather_rows(w_inner.astype(BF16))
    full_outer_t = gather_rows(w_outer.T.astype(BF16))

    qkv = dot(hidden, full_qkv).astype(BF16)
    own_kv = qkv[:, local:]
    ctx = lax.axis_size("ctx")
    edges = Once(
        along(own_kv[length - REACH :], "ctx", upward(0, ctx - 1)),
        along(own_kv[:REACH], "ctx", downward(1, ctx)),
    )
    step([edges])
    padded_kv = jnp.concatenate([edges.got[0], own_kv, edges.got[1]], axis=0)

    position = jnp.arange(length, dtype=jnp.int32)
    anchor = lax.axis_index("ctx") * length - REACH
    low = jnp.maximum(doc_span[0] - anchor, position[None])
    high = jnp.minimum(doc_span[1] - anchor, position[None] + 2 * REACH)
    attended = attend(low, high, qkv, padded_kv, heads)

    all_heads = Gather(attended, "tp")
    mom_outer_t, mom_out_t = step([all_heads], lambda a, b: (a.T, b.T), mom_outer, mom_out)
    for _ in range(tp - 2):
        step([all_heads])
    head_slots = all_heads.slots()

    order = slot_order(tp)
    first, rest = order[:2], order[2:]
    normed_slots, pre_slots, act_slots, parts = ([None] * tp for _ in range(4))
    def forward(r):
        attended_r = jnp.concatenate([slice_of(slot, r) for slot in head_slots], axis=1)
        branch = dot_nt(attended_r, full_out_t)
        unit, scale = normalize(slice_of(hidden, r).astype(F32) + branch)
        normed = unit * norm_gains[0] + norm_biases[0]
        normed_slots[r] = normed.astype(BF16)
        pre_slots[r] = dot(normed_slots[r], full_inner)
        act_slots[r] = gelu_tanh(pre_slots[r]).astype(BF16)
        return unit, scale, normed

    def terms_of(slots, *acts):
        return [
            dot_nt(act, full_outer_t).astype(F32 if r == 0 else BF16) for r, act in zip(slots, acts)
        ]

    for r in order:
        unit_one, scale_one, own_normed = forward(r)
    for r, value in zip(first, terms_of(first, *[act_slots[r] for r in first])):
        parts[r] = value
    ffn_sum = Scatter(parts, "tp")
    acts = [act_slots[r] for r in rest]
    for r, value in zip(rest, step([ffn_sum], functools.partial(terms_of, rest), *acts)):
        parts[r] = value

    def slopes_of(*pres):
        return [jax.vjp(gelu_tanh, pre)[1](jnp.ones_like(pre))[0] for pre in pres]

    slopes = [None] * tp
    half = tp // 2
    slopes[:half] = step([ffn_sum], slopes_of, *pre_slots[:half])
    slopes[half:] = step([ffn_sum], slopes_of, *pre_slots[half:])
    for _ in range(tp - 4):
        step([ffn_sum])

    unit_two, scale_two = normalize(own_normed + ffn_sum.total())
    own_out = (unit_two * norm_gains[1] + norm_biases[1]).astype(BF16)
    seed = slice_of(cotangent[0], 0).astype(F32)
    grad_two, gain_two, shift_two = norm_backward(seed, unit_two, scale_two, norm_gains[1])
    dffn_all = Gather(grad_two.astype(BF16), "tp")
    dpre_slots, parts = [None] * tp, [None] * tp

    def backward(*pairs):
        made = []
        for dffn, slope in pairs:
            dpre = (dot(dffn, full_outer_t) * slope).astype(BF16)
            made.append((dpre, dot_nt(dpre, full_inner).astype(BF16)))
        return made

    def keep_back(slots, made):
        for r, values in zip(slots, made):
            dpre_slots[r], parts[r] = values

    step([dffn_all])
    keep_back([0], step([dffn_all], backward, (dffn_all.slot(0), slopes[0])))
    middle = [r for r in rest if r]
    ready = [(dffn_all.slot(r), slopes[r]) for r in middle] if tp == 4 else []
    made = step([dffn_all], backward, *ready)
    for _ in range(tp - 4):
        step([dffn_all])
    if not ready:
        made = backward(*[(dffn_all.slot(r), slopes[r]) for r in middle])
    keep_back(middle, made)
    dffn_slots = dffn_all.slots()
    out_all = Gather(own_out, "tp")
    keep_back(first, step([out_all], backward, *[(dffn_slots[r], slopes[r]) for r in first]))

    dnormed_sum = Scatter(parts, "tp")

    def weight_grad(lefts, rights):
        return dot_tn(jnp.concatenate(lefts, axis=0), jnp.concatenate(rights, axis=0)).astype(BF16)

    grad_outer_t = step([out_all, dnormed_sum], weight_grad, dffn_slots, act_slots)
    grad_outer_t = scatter_rows(grad_outer_t)
    grad_inner = step([out_all, dnormed_sum], weight_grad, normed_slots, dpre_slots)
    grad_inner = scatter_rows(grad_inner)
    layer_out = step([dnormed_sum], lambda *slots: placed(slots, BF16, me), *out_all.terms())[None]
    for _ in range(tp - 4):
        step([dnormed_sum])
    dnormed = grad_two + dnormed_sum.total()

    grad_one, gain_one, shift_one = norm_backward(dnormed, unit_one, scale_one, norm_gains[0])
    dbranch_low = grad_one.astype(BF16)
    dattended_all = dot(dbranch_low, full_out_t).astype(BF16)
    blocks = [dattended_all[:, (-r % tp) * local : (-r % tp + 1) * local] for r in range(tp)]
    dattended = Exchange(blocks, "tp")
    sums = jnp.stack([gain_one, gain_two, shift_one, shift_two])
    step([dattended])
    part = width // tp
    dbranch = Exchange(
        [
            lax.dynamic_slice_in_dim(dbranch_low, lax.rem(me + r, tp) * part, part, 1)
            for r in range(tp)
        ],
        "tp",
    )

    def attention_back(*slots):
        return attend_back(low, high, qkv, padded_kv, placed([[slot] for slot in slots], BF16, me), heads)

    dq_low, key_grad, value_grad = step([dbranch], attention_back, *dattended.slots)

    def kv_rows(start, count):
        rows = slice(start, start + count)
        return jnp.concatenate([key_grad[rows], value_grad[rows]], axis=1)

    edges = Once(
        along(kv_rows(0, REACH).astype(BF16), "ctx", downward(1, ctx)),
        along(kv_rows(length + REACH, REACH).astype(BF16), "ctx", upward(0, ctx - 1)),
    )
    rows = w_query.shape[0]
    group = width // rows

    def out_pieces(dbranch_slots, head_slots):
        columns = placed([[slot] for slot in dbranch_slots], BF16, me)
        sums = [dot_tn(columns, slot).astype(BF16).reshape(-1, rows, local) for slot in head_slots]
        return row_major(jnp.stack(sums, axis=1).reshape(group * rows, local))

    pieces = step([edges], out_pieces, dbranch.slots, head_slots)
    from_above, from_below = (edge.astype(F32) for edge in edges.got)
    beyond = length - REACH
    added = jnp.pad(from_above, ((beyond, 0), (0, 0))) + jnp.pad(from_below, ((0, beyond), (0, 0)))
    dqkv = jnp.concatenate([dq_low, (kv_rows(REACH, length) + added).astype(BF16)], axis=1)
    grad_attn = row_major(jnp.concatenate([dot_tn(hidden, dqkv).astype(BF16), pieces], axis=1))
    dqkv = after(dqkv, grad_attn)
    grad_attn = scatter_rows(grad_attn)

    parts = [None] * tp

    def input_terms(slots, dqkv):
        rows = jnp.concatenate([slice_of(dqkv, r) for r in slots], axis=0)
        sums = dot_nt(rows, full_qkv).astype(BF16)
        return [sums[n * share : (n + 1) * share] for n in range(len(slots))]

    for r, value in zip(first, input_terms(first, dqkv)):
        parts[r] = value
    input_sum = Scatter(parts, "tp")

    def between(dqkv, grad_inner, grad_outer_t):
        moments = blend(mom_inner, grad_inner), blend(mom_outer_t, grad_outer_t)
        blocks = to_owners(sum(map(column_blocks, moments), []))
        return input_terms(rest, dqkv), moments, blocks

    terms, (moment_inner, moment_outer_t), blocks = step(
        [input_sum], between, dqkv, grad_inner, grad_outer_t
    )
    grad_inner, grad_outer_t = grad_inner.astype(F32), grad_outer_t.astype(F32)
    for r, value in zip(rest, terms):
        parts[r] = value
    owners = Once(swapped(blocks))
    grad_outer, moment_outer = step(
        [input_sum, owners], lambda a, b: (a.T, b.T), grad_outer_t, moment_outer_t
    )
    homes = [
        (p * tp + t, (t * (group // tp) + p // tp) * tp + (t - p % tp) % tp)
        for p in range(group)
        for t in range(tp)
    ]
    piece = Once(along(grad_attn[:, 3 * local :], (*WEIGHT_AXES, "tp"), homes))
    iterate, grad_qkv, sums = step(
        [input_sum, piece],
        lambda owned, *values: (orthogonal_start(owned), *values),
        owners.got[0],
        grad_attn[:, : 3 * local],
        sums,
    )
    totals = jnp.sum(lax.all_gather(sums, (*WEIGHT_AXES, "tp"), axis=0), axis=0)
    for _ in range(tp - 4):
        step([input_sum])
    own_input = Gather((grad_one + input_sum.total()).astype(BF16), "tp")

    grad_query, grad_key, grad_value = jnp.split(grad_qkv.astype(F32), 3, axis=1)
    grad_out_t = row_major(piece.got[0]).astype(F32)
    moment_query = blend(mom_query, grad_query)
    moment_key = blend(mom_key, grad_key)
    moment_value = blend(mom_value, grad_value)
    moment_out_t = blend(mom_out_t, grad_out_t)
    moments = moment_query, moment_key, moment_value, moment_out_t
    shard = lax.axis_size("shard")
    at_shard = lax.axis_index("shard")
    blocks = [row_major(m.astype(BF16)) for m in sum(map(column_blocks, moments), [])]
    blocks = row_major(jnp.stack(blocks))
    blocks = blocks.reshape(shard, -1, *blocks.shape[1:])

    def turned(value, r):
        return lax.dynamic_index_in_dim(value, lax.rem(at_shard + r, shard), 0, keepdims=False)

    owners = Exchange([turned(blocks, r)[0] for r in range(shard)], "shard")
    finish = functools.partial(orthogonal_end, group=group)
    step([owners])
    mine = row_major(jnp.stack(owners.slots))
    peers = Once(
        *[along(mine, "ctx", [(i, (i + by) % ctx) for i in range(ctx)]) for by in range(1, ctx)]
    )
    done = step([own_input, peers], finish, iterate)
    owned = jnp.concatenate([mine, *peers.got], axis=0)

    def update_ffn(back):
        ortho = from_owners(back, 2 * moment_inner.shape[1] // BW)
        half = len(ortho) // 2
        return (
            w_inner - MATRIX_RATE * jnp.concatenate(ortho[:half], axis=1),
            w_outer - MATRIX_RATE * jnp.concatenate(ortho[half:], axis=1).T,
        )

    ortho = Once(swapped(done))
    iterate = step([own_input, ortho], orthogonal_start, owned)
    done = row_major(step([own_input], finish, iterate))
    for _ in range(tp - 4):
        step([own_input])
    attn = Once(
        *[
            along(done[r], "shard", [(i, (i - r) % shard) for i in range(shard)])
            for r in range(1, shard)
        ]
    )

    def closing(back, *slots):
        return update_ffn(back), placed(slots, F32, me)

    (new_inner, new_outer), input_grad = step([attn], closing, ortho.got[0], *own_input.terms())
    input_grad = input_grad[None]
    ortho = row_major(jnp.stack([done[0], *map(row_major, attn.got)]))
    ortho = [
        lax.dynamic_index_in_dim(ortho, lax.rem(b - at_shard + shard, shard), 0, keepdims=False)
        for b in range(shard)
    ]
    ortho = [row_major(block).astype(F32) for block in ortho]
    gain_grad, bias_grad = totals[:2], totals[2:]
    new_query = w_query - MATRIX_RATE * ortho[0]
    new_key = w_key - MATRIX_RATE * ortho[1]
    new_value = w_value - MATRIX_RATE * ortho[2]
    new_out = w_out - MATRIX_RATE * ortho[3].T

    tokens_all = length * lax.axis_size("shard") * ctx
    gain_moment_new = blend(gain_moment, gain_grad)
    bias_moment_new = blend(bias_moment, bias_grad)
    new_gains = norm_gains - VECTOR_RATE * gain_moment_new / math.sqrt(tokens_all)
    new_biases = norm_biases - VECTOR_RATE * bias_moment_new / math.sqrt(tokens_all)
    return (
        layer_out,
        input_grad,
        grad_query,
        grad_key,
        grad_value,
        grad_out_t.T,
        grad_inner,
        grad_outer,
        gain_grad,
        bias_grad,
        moment_query,
        moment_key,
        moment_value,
        moment_out_t.T,
        moment_inner,
        moment_outer,
        gain_moment_new,
        bias_moment_new,
        new_query,
        new_key,
        new_value,
        new_out,
        new_inner,
        new_outer,
        new_gains,
        new_biases,
    )


def solution(mesh):
    tokens = P("shard", "ctx", None)
    by_rows = P(WEIGHT_AXES, "tp")
    by_columns = P("tp", WEIGHT_AXES)
    matrices = (by_rows, by_rows, by_rows, by_columns, by_rows, by_columns)
    return jax.shard_map(
        body,
        mesh=mesh,
        in_specs=(tokens, P(None, "shard", "ctx"), tokens, *matrices, P(), P(), *matrices, P(), P()),
        out_specs=(tokens, tokens, *matrices, P(), P(), *matrices, P(), P(), *matrices, P(), P()),
        check_vma=False,
    )
```

```python
import functools
import math

import jax
import jax.numpy as jnp
from jax import lax
from jax.experimental import pallas as pl
from jax.experimental.layout import Layout, with_layout_constraint
from jax.experimental.pallas import tpu as pltpu
from jax.sharding import PartitionSpec as P

HEAD_DIM = 128
REACH = 512
BW = 512
NS_STEPS = 5
QUERY_ROWS = 256

NS_COEFFS = (3.4445, -4.775, 2.0315)
LN_EPSILON = 1e-12
BETA = 0.5
MATRIX_RATE = 0.5
VECTOR_RATE = 0.3
MASKED = -1e30
WEIGHT_AXES = ("shard", "ctx")
BF16 = jnp.bfloat16
F32 = jnp.float32


def along(value, axis, pairs):
    return value, functools.partial(lax.ppermute, axis_name=axis, perm=pairs)


def upward(first, last):
    return [(i, i + 1) for i in range(first, last)]


def downward(first, last):
    return [(i, i - 1) for i in range(first, last)]


class Gather:
    def __init__(self, block, axis):
        self.count, self.axis = lax.axis_size(axis), axis
        self.block, self.ups, self.downs = block, [], []

    def sends(self):
        step = len(self.ups) + 1
        up, down = (self.ups[-1], self.downs[-1]) if self.ups else (self.block, self.block)
        return [
            along(up, self.axis, upward(step - 1, self.count - 1)),
            along(down, self.axis, downward(1, self.count - step + 1)),
        ]

    def take(self, got):
        self.ups.append(got[0])
        self.downs.append(got[1])

    def slot(self, r):
        return self.ups[r - 1] + self.downs[self.count - r - 1] if r else self.block

    def slots(self):
        return [self.slot(r) for r in range(self.count)]

    def terms(self):
        pairs = [[self.ups[r - 1], self.downs[self.count - r - 1]] for r in range(1, self.count)]
        return [[self.block], *pairs]


class Scatter:
    def __init__(self, parts, axis):
        self.count, self.axis = lax.axis_size(axis), axis
        self.parts, self.step, self.got = parts, 0, None

    def sends(self):
        self.step += 1
        step, count = self.step, self.count
        terms = [self.parts[step], self.parts[count - step]]
        if self.got:
            terms = [
                term.astype(F32) + got.astype(F32) for term, got in zip(terms, self.got)
            ]
        return [
            along(terms[0].astype(BF16), self.axis, upward(0, step)),
            along(terms[1].astype(BF16), self.axis, downward(count - step, count)),
        ]

    def take(self, got):
        self.got = got

    def total(self):
        return self.parts[0].astype(F32) + (self.got[0].astype(F32) + self.got[1].astype(F32))


class Exchange:
    def __init__(self, blocks, axis):
        self.blocks, self.axis = blocks, axis

    def sends(self):
        count = len(self.blocks)
        return [
            along(self.blocks[r], self.axis, [(i, (i + r) % count) for i in range(count)])
            for r in range(1, count)
        ]

    def take(self, got):
        self.slots = [self.blocks[0], *got]


class Once:
    def __init__(self, *sends):
        self.all = list(sends)

    def sends(self):
        return self.all

    def take(self, got):
        self.got = got


def step(movers, work=None, *operands):
    sends = [mover.sends() for mover in movers]
    values = [[value for value, _ in group] for group in sends]
    values, operands = lax.optimization_barrier((values, operands))
    got = [
        [send(value) for value, (_, send) in zip(vals, group)] for vals, group in zip(values, sends)
    ]
    done = work(*operands) if work else ()
    got, done = lax.optimization_barrier((got, done))
    for mover, arrived in zip(movers, got):
        mover.take(arrived)
    return done


def slot_order(count):
    order = []
    for hop in range(1, count):
        order += [r for r in dict.fromkeys((hop, count - hop)) if r not in order]
    return order + [0]


def after(value, *others):
    return lax.optimization_barrier((value, *others))[0]


def row_major(value):
    return with_layout_constraint(value, Layout(major_to_minor=tuple(range(value.ndim))))


def dot(left, right):
    return jnp.dot(left, right, preferred_element_type=F32)


def dot_nt(left, right):
    return lax.dot_general(left, right, (((1,), (1,)), ((), ())), preferred_element_type=F32)


def dot_tn(left, right):
    return lax.dot_general(left, right, (((0,), (0,)), ((), ())), preferred_element_type=F32)


def normalize(hidden):
    centred = hidden - jnp.mean(hidden, axis=-1, keepdims=True)
    variance = jnp.mean(centred * centred, axis=-1, keepdims=True)
    scale = lax.rsqrt(variance + LN_EPSILON)
    return centred * scale, scale


def norm_backward(grad, unit, scale, gain):
    scaled = grad * gain
    inner = jnp.mean(scaled * unit, axis=-1, keepdims=True)
    dhidden = scale * (scaled - jnp.mean(scaled, axis=-1, keepdims=True) - unit * inner)
    return dhidden, jnp.sum(grad * unit, axis=0), jnp.sum(grad, axis=0)


def gelu_tanh(values):
    return jax.nn.gelu(values, approximate=True)


def window_probs(q, keys, low_ref, high_ref, start):
    scores = dot_nt(keys, q) * (HEAD_DIM**-0.5)
    at = start + lax.broadcasted_iota(jnp.int32, scores.shape, 0)
    scores = jnp.where((at >= low_ref[...]) & (at <= high_ref[...]), scores, MASKED)
    expo = jnp.exp(scores - jnp.max(scores, axis=0, keepdims=True))
    return expo * (1.0 / jnp.sum(expo, axis=0, keepdims=True))


def attend_kernel(low_ref, high_ref, q_ref, k_ref, v_ref, o_ref):
    rows = q_ref.shape[0]
    span = rows + 2 * REACH
    start = pl.multiple_of(pl.program_id(1) * rows, rows)
    probs = window_probs(q_ref[...], k_ref[pl.ds(start, span), :], low_ref, high_ref, start)
    o_ref[...] = dot_tn(probs.astype(BF16), v_ref[pl.ds(start, span), :]).astype(BF16)


def attend_back_kernel(
    low_ref, high_ref, q_ref, k_ref, v_ref, g_ref, dq_ref, above_ref, centre_ref, below_ref, total
):
    rows = q_ref.shape[0]
    span = rows + 2 * REACH
    start = pl.multiple_of(pl.program_id(1) * rows, rows)
    window = pl.ds(start, span)

    @pl.when(pl.program_id(1) == 0)
    def _():
        total[...] = jnp.zeros_like(total)

    q, g, keys = q_ref[...], g_ref[...], k_ref[window, :]
    probs = window_probs(q, keys, low_ref, high_ref, start)
    dprobs = dot_nt(v_ref[window, :], g)
    offset = jnp.sum(dprobs * probs, axis=0, keepdims=True)
    dscores = (probs * (dprobs - offset) * (HEAD_DIM**-0.5)).astype(BF16)
    total[1, window, :] += dot(probs.astype(BF16), g)
    total[0, window, :] += dot(dscores, q)
    dq_ref[...] = dot_tn(dscores, keys).astype(BF16)

    @pl.when(pl.program_id(1) == pl.num_programs(1) - 1)
    def _():
        length = centre_ref.shape[1]
        above_ref[...] = total[:, :REACH, :].astype(BF16)
        centre_ref[...] = total[:, REACH : REACH + length, :]
        below_ref[...] = total[:, REACH + length :, :].astype(BF16)


def attention_specs(rows, padded, heads):
    bounds = pl.BlockSpec((1, rows), lambda h, b: (0, b))
    queries = pl.BlockSpec((rows, HEAD_DIM), lambda h, b: (b, h))
    keys = pl.BlockSpec((padded, HEAD_DIM), lambda h, b: (0, h))
    values = pl.BlockSpec((padded, HEAD_DIM), lambda h, b: (0, h + heads))
    return bounds, queries, keys, values


def attend(low, high, qkv, padded_kv, heads):
    length, padded = qkv.shape[0], padded_kv.shape[0]
    rows = min(QUERY_ROWS, length)
    bounds, q_spec, k_spec, v_spec = attention_specs(rows, padded, heads)
    pairs = heads * length * (rows + 2 * REACH)
    return pl.pallas_call(
        attend_kernel,
        grid=(heads, length // rows),
        in_specs=[bounds, bounds, q_spec, k_spec, v_spec],
        out_specs=q_spec,
        out_shape=jax.ShapeDtypeStruct((length, heads * HEAD_DIM), BF16),
        cost_estimate=pl.CostEstimate(
            flops=16 * pairs * HEAD_DIM, transcendentals=pairs, bytes_accessed=8 << 20
        ),
        name="attend",
    )(low, high, qkv, padded_kv, padded_kv)


def attend_back(low, high, qkv, padded_kv, grads, heads):
    length, padded = qkv.shape[0], padded_kv.shape[0]
    rows = min(QUERY_ROWS, length)
    bounds, q_spec, k_spec, v_spec = attention_specs(rows, padded, heads)
    pairs = heads * length * (rows + 2 * REACH)
    width = heads * HEAD_DIM

    def stacked(count):
        return pl.BlockSpec((2, count, HEAD_DIM), lambda h, b: (0, 0, h))

    return pl.pallas_call(
        attend_back_kernel,
        grid=(heads, length // rows),
        in_specs=[bounds, bounds, q_spec, k_spec, v_spec, q_spec],
        out_specs=(q_spec, stacked(REACH), stacked(length), stacked(REACH)),
        out_shape=(
            jax.ShapeDtypeStruct((length, width), BF16),
            jax.ShapeDtypeStruct((2, REACH, width), BF16),
            jax.ShapeDtypeStruct((2, length, width), F32),
            jax.ShapeDtypeStruct((2, REACH, width), BF16),
        ),
        scratch_shapes=[pltpu.VMEM((2, padded, HEAD_DIM), F32)],
        cost_estimate=pl.CostEstimate(
            flops=32 * pairs * HEAD_DIM, transcendentals=pairs, bytes_accessed=20 << 20
        ),
        name="attend_back",
    )(low, high, qkv, padded_kv, padded_kv, grads)


def place_kernel(sizes, me_ref, *refs):
    at = 0
    for r, size in enumerate(sizes):
        terms = refs[at : at + size]
        at += size

        @pl.when(pl.program_id(0) == r)
        def _(terms=terms):
            value = terms[0][...]
            for term in terms[1:]:
                value = value + term[...]
            refs[-1][...] = value.astype(refs[-1].dtype)


def placed(slots, dtype, me):
    count = len(slots)
    share, width = slots[0][0].shape
    flat = [term for slot in slots for term in slot]
    whole = pl.BlockSpec((share, width), lambda r, me_ref: (0, 0))
    return pl.pallas_call(
        functools.partial(place_kernel, [len(slot) for slot in slots]),
        grid_spec=pltpu.PrefetchScalarGridSpec(
            num_scalar_prefetch=1,
            grid=(count,),
            in_specs=[whole] * len(flat),
            out_specs=pl.BlockSpec(
                (share, width), lambda r, me_ref: (lax.rem(me_ref[0] - r + count, count), 0)
            ),
        ),
        out_shape=jax.ShapeDtypeStruct((count * share, width), dtype),
        cost_estimate=pl.CostEstimate(
            flops=0, transcendentals=0, bytes_accessed=6 * count * share * width
        ),
        name="place",
    )(me.reshape(1), *flat)


def halves(value):
    top = value.astype(BF16)
    return top, (value - top.astype(F32)).astype(BF16)


def newton_schulz_kernel(steps, in_ref, out_ref, top, rest, iterate=None):
    opening = iterate is None
    iterate = out_ref if opening else iterate
    depth = top.shape[1]
    chunk = min(1024, depth)
    chunks = depth // chunk

    def columns(c):
        return pl.ds(pl.multiple_of(c * chunk, chunk), chunk)

    def load(c, total):
        part = in_ref[columns(c), :].astype(F32)
        iterate[:, columns(c)] = part.T
        return total + jnp.sum(part * part, axis=(0, 1), keepdims=True)

    if opening:
        norm = jnp.sqrt(lax.fori_loop(0, chunks, load, jnp.zeros((1, 1), F32)))
        inverse = 1.0 / (norm + 1e-07)

    def split(c, carry):
        value = iterate[:, columns(c)] * inverse if opening else in_ref[:, columns(c)]
        iterate[:, columns(c)] = value
        top[:, columns(c)], rest[:, columns(c)] = halves(value)
        return carry

    lax.fori_loop(0, chunks, split, 0)

    def step(index, carry):
        gram = dot_nt(top[...], top[...])
        gram_top, gram_rest = halves(gram)
        cross = dot(gram_top, gram_rest)
        square = dot(gram_top, gram_top) + (cross + cross.T)
        poly_top, poly_rest = halves(NS_COEFFS[1] * gram + NS_COEFFS[2] * square)

        def update(c, carry):
            here = columns(c)
            change = dot(poly_top, top[:, here]) + dot(poly_rest, top[:, here])
            value = NS_COEFFS[0] * iterate[:, here] + (change + dot(poly_top, rest[:, here]))
            iterate[:, here] = value
            top[:, here], rest[:, here] = halves(value)
            return carry

        return lax.fori_loop(0, chunks, update, carry)

    lax.fori_loop(0, steps, step, 0)

    def store(c, carry):
        out_ref[columns(c), :] = iterate[:, columns(c)].T.astype(BF16)
        return carry

    if not opening:
        lax.fori_loop(0, chunks, store, 0)


def newton_schulz_part(steps, value, out, depth, width, scratch):
    return pl.pallas_call(
        functools.partial(newton_schulz_kernel, steps),
        out_shape=out,
        in_specs=[pl.BlockSpec(memory_space=pltpu.VMEM)],
        out_specs=pl.BlockSpec(memory_space=pltpu.VMEM),
        scratch_shapes=[pltpu.VMEM((width, depth), BF16), pltpu.VMEM((width, depth), BF16), *scratch],
        cost_estimate=pl.CostEstimate(
            flops=2 * steps * width * width * (4 * depth + 2 * width),
            transcendentals=0,
            bytes_accessed=6 * depth * width,
        ),
        name="newton_schulz",
    )(value)


def orthogonal_start(owned):
    depth, width = owned.shape[0] * owned.shape[1], owned.shape[2]
    out = jax.ShapeDtypeStruct((width, depth), F32)
    return newton_schulz_part(NS_STEPS // 2, owned.reshape(depth, width), out, depth, width, [])


def orthogonal_end(iterate, group):
    width, depth = iterate.shape
    out = jax.ShapeDtypeStruct((depth, width), BF16)
    scratch = [pltpu.VMEM((width, depth), F32)]
    done = newton_schulz_part(NS_STEPS - NS_STEPS // 2, iterate, out, depth, width, scratch)
    return done.reshape(group, depth // group, width)


def to_owners(blocks):
    copies = lax.axis_size("shard") * lax.axis_size("ctx") // len(blocks)
    return jnp.stack([block.astype(BF16) for block in blocks for _ in range(copies)])


def swapped(value):
    return value, functools.partial(
        lax.all_to_all, axis_name=WEIGHT_AXES, split_axis=0, concat_axis=0, tiled=True
    )


def from_owners(back, count):
    copies = back.shape[0] // count
    return [back[b * copies].astype(F32) for b in range(count)]


def column_blocks(value):
    return [value[:, at : at + BW] for at in range(0, value.shape[1], BW)]


def turn_kernel(grad_ref, old_ref, out_ref, moment_ref):
    turned = grad_ref[...].astype(F32).T
    out_ref[...] = turned
    moment_ref[...] = BETA * old_ref[...] + (1.0 - BETA) * turned


def turned_moment(grad_t, old):
    rows, width = grad_t.shape
    here = pl.BlockSpec((BW, rows), lambda j: (j, 0))
    out = jax.ShapeDtypeStruct((width, rows), F32)
    return pl.pallas_call(
        turn_kernel,
        grid=(width // BW,),
        in_specs=[pl.BlockSpec((rows, BW), lambda j: (0, j)), here],
        out_specs=(here, here),
        out_shape=(out, out),
        cost_estimate=pl.CostEstimate(
            flops=3 * rows * width, transcendentals=0, bytes_accessed=14 * rows * width
        ),
        name="turn",
    )(grad_t, old)


def update_kernel(ortho_ref, old_ref, out_ref):
    out_ref[...] = old_ref[...] - MATRIX_RATE * ortho_ref[...].astype(F32).T


def turned_update(back, first, copies, old):
    width, rows = old.shape
    here = pl.BlockSpec((BW, rows), lambda j: (j, 0))
    return pl.pallas_call(
        update_kernel,
        grid=(width // BW,),
        in_specs=[pl.BlockSpec((None, rows, BW), lambda j: ((first + j) * copies, 0, 0)), here],
        out_specs=here,
        out_shape=jax.ShapeDtypeStruct((width, rows), F32),
        cost_estimate=pl.CostEstimate(
            flops=2 * rows * width, transcendentals=0, bytes_accessed=10 * rows * width
        ),
        name="update",
    )(back, old)


def gather_rows(value):
    return lax.all_gather(value, WEIGHT_AXES, axis=0, tiled=True)


def scatter_rows(value):
    return lax.psum_scatter(value, WEIGHT_AXES, scatter_dimension=0, tiled=True)


def blend(old, grad):
    return BETA * old + (1.0 - BETA) * grad


def body(
    hidden_in,
    doc_span,
    cotangent,
    w_query,
    w_key,
    w_value,
    w_out,
    w_inner,
    w_outer,
    norm_gains,
    norm_biases,
    mom_query,
    mom_key,
    mom_value,
    mom_out,
    mom_inner,
    mom_outer,
    gain_moment,
    bias_moment,
):
    tp = lax.axis_size("tp")
    me = lax.axis_index("tp")
    hidden = hidden_in[0]
    length, width = hidden.shape
    share = length // tp
    local = w_query.shape[1]
    heads = local // HEAD_DIM

    def slice_of(value, r):
        return lax.dynamic_slice_in_dim(value, lax.rem(me - r + tp, tp) * share, share, 0)

    full_qkv = gather_rows(jnp.concatenate([w_query, w_key, w_value], axis=1).astype(BF16))
    w_out_t = Gather(w_out.T.astype(BF16), "tp")
    for _ in range(tp - 1):
        step([w_out_t])
    full_out_t = gather_rows(jnp.concatenate(w_out_t.slots(), axis=1))
    full_inner = gather_rows(w_inner.astype(BF16))
    full_outer_t = gather_rows(w_outer.T.astype(BF16))

    qkv = dot(hidden, full_qkv).astype(BF16)
    own_kv = qkv[:, local:]
    ctx = lax.axis_size("ctx")
    edges = Once(
        along(own_kv[length - REACH :], "ctx", upward(0, ctx - 1)),
        along(own_kv[:REACH], "ctx", downward(1, ctx)),
    )
    step([edges])
    padded_kv = jnp.concatenate([edges.got[0], own_kv, edges.got[1]], axis=0)

    position = jnp.arange(length, dtype=jnp.int32)
    anchor = lax.axis_index("ctx") * length - REACH
    low = jnp.maximum(doc_span[0] - anchor, position[None])
    high = jnp.minimum(doc_span[1] - anchor, position[None] + 2 * REACH)
    attended = attend(low, high, qkv, padded_kv, heads)

    all_heads = Gather(attended, "tp")
    mom_outer_t, mom_out_t = step([all_heads], lambda a, b: (a.T, b.T), mom_outer, mom_out)
    for _ in range(tp - 2):
        step([all_heads])
    head_slots = all_heads.slots()

    order = slot_order(tp)
    first, rest = order[:2], order[2:]
    normed_slots, pre_slots, act_slots, parts = ([None] * tp for _ in range(4))
    def forward(r):
        attended_r = jnp.concatenate([slice_of(slot, r) for slot in head_slots], axis=1)
        branch = dot_nt(attended_r, full_out_t)
        unit, scale = normalize(slice_of(hidden, r).astype(F32) + branch)
        normed = unit * norm_gains[0] + norm_biases[0]
        normed_slots[r] = normed.astype(BF16)
        pre_slots[r] = dot(normed_slots[r], full_inner)
        act_slots[r] = gelu_tanh(pre_slots[r]).astype(BF16)
        return unit, scale, normed

    def terms_of(slots, *acts):
        return [
            dot_nt(act, full_outer_t).astype(F32 if r == 0 else BF16) for r, act in zip(slots, acts)
        ]

    for r in order:
        unit_one, scale_one, own_normed = forward(r)
    for r, value in zip(first, terms_of(first, *[act_slots[r] for r in first])):
        parts[r] = value
    ffn_sum = Scatter(parts, "tp")
    acts = [act_slots[r] for r in rest]
    for r, value in zip(rest, step([ffn_sum], functools.partial(terms_of, rest), *acts)):
        parts[r] = value

    def slopes_of(*pres):
        return [jax.vjp(gelu_tanh, pre)[1](jnp.ones_like(pre))[0] for pre in pres]

    slopes = [None] * tp
    half = tp // 2
    slopes[:half] = step([ffn_sum], slopes_of, *pre_slots[:half])
    slopes[half:] = step([ffn_sum], slopes_of, *pre_slots[half:])
    for _ in range(tp - 4):
        step([ffn_sum])

    unit_two, scale_two = normalize(own_normed + ffn_sum.total())
    own_out = (unit_two * norm_gains[1] + norm_biases[1]).astype(BF16)
    seed = slice_of(cotangent[0], 0).astype(F32)
    grad_two, gain_two, shift_two = norm_backward(seed, unit_two, scale_two, norm_gains[1])
    dffn_all = Gather(grad_two.astype(BF16), "tp")
    dpre_slots, parts = [None] * tp, [None] * tp

    def backward(*pairs):
        made = []
        for dffn, slope in pairs:
            dpre = (dot(dffn, full_outer_t) * slope).astype(BF16)
            made.append((dpre, dot_nt(dpre, full_inner).astype(BF16)))
        return made

    def keep_back(slots, made):
        for r, values in zip(slots, made):
            dpre_slots[r], parts[r] = values

    step([dffn_all])
    keep_back([0], step([dffn_all], backward, (dffn_all.slot(0), slopes[0])))
    middle = [r for r in rest if r]
    ready = [(dffn_all.slot(r), slopes[r]) for r in middle] if tp == 4 else []
    made = step([dffn_all], backward, *ready)
    for _ in range(tp - 4):
        step([dffn_all])
    if not ready:
        made = backward(*[(dffn_all.slot(r), slopes[r]) for r in middle])
    keep_back(middle, made)
    dffn_slots = dffn_all.slots()
    out_all = Gather(own_out, "tp")
    keep_back(first, step([out_all], backward, *[(dffn_slots[r], slopes[r]) for r in first]))

    dnormed_sum = Scatter(parts, "tp")

    def weight_grad(lefts, rights):
        return dot_tn(jnp.concatenate(lefts, axis=0), jnp.concatenate(rights, axis=0)).astype(BF16)

    grad_outer_t = step([out_all, dnormed_sum], weight_grad, dffn_slots, act_slots)
    grad_outer_t = scatter_rows(grad_outer_t)
    grad_inner = step([out_all, dnormed_sum], weight_grad, normed_slots, dpre_slots)
    grad_inner = scatter_rows(grad_inner)
    layer_out = step([dnormed_sum], lambda *slots: placed(slots, BF16, me), *out_all.terms())[None]
    for _ in range(tp - 4):
        step([dnormed_sum])
    dnormed = grad_two + dnormed_sum.total()

    grad_one, gain_one, shift_one = norm_backward(dnormed, unit_one, scale_one, norm_gains[0])
    dbranch_low = grad_one.astype(BF16)
    dattended_all = dot(dbranch_low, full_out_t).astype(BF16)
    blocks = [dattended_all[:, (-r % tp) * local : (-r % tp + 1) * local] for r in range(tp)]
    dattended = Exchange(blocks, "tp")
    sums = jnp.stack([gain_one, gain_two, shift_one, shift_two])
    step([dattended])
    part = width // tp
    dbranch = Exchange(
        [
            lax.dynamic_slice_in_dim(dbranch_low, lax.rem(me + r, tp) * part, part, 1)
            for r in range(tp)
        ],
        "tp",
    )

    def attention_back(*slots):
        return attend_back(low, high, qkv, padded_kv, placed([[slot] for slot in slots], BF16, me), heads)

    dq_low, kv_above, kv_centre, kv_below = step([dbranch], attention_back, *dattended.slots)
    edges = Once(
        along(kv_above, "ctx", downward(1, ctx)), along(kv_below, "ctx", upward(0, ctx - 1))
    )
    rows = w_query.shape[0]
    group = width // rows

    def out_pieces(dbranch_slots, head_slots):
        columns = placed([[slot] for slot in dbranch_slots], BF16, me)
        sums = [dot_tn(columns, slot).astype(BF16).reshape(-1, rows, local) for slot in head_slots]
        return row_major(jnp.stack(sums, axis=1).reshape(group * rows, local))

    pieces = step([edges], out_pieces, dbranch.slots, head_slots)
    from_above, from_below = (edge.astype(F32) for edge in edges.got)
    beyond = length - REACH
    added = jnp.pad(from_above, ((0, 0), (beyond, 0), (0, 0))) + jnp.pad(
        from_below, ((0, 0), (0, beyond), (0, 0))
    )
    kv_low = (kv_centre + added).astype(BF16)
    dqkv = jnp.concatenate([dq_low, kv_low[0], kv_low[1]], axis=1)
    grad_attn = row_major(jnp.concatenate([dot_tn(hidden, dqkv).astype(BF16), pieces], axis=1))
    dqkv = after(dqkv, grad_attn)
    grad_attn = scatter_rows(grad_attn)

    parts = [None] * tp

    def input_terms(slots, dqkv):
        rows = jnp.concatenate([slice_of(dqkv, r) for r in slots], axis=0)
        sums = dot_nt(rows, full_qkv).astype(BF16)
        return [sums[n * share : (n + 1) * share] for n in range(len(slots))]

    for r, value in zip(first, input_terms(first, dqkv)):
        parts[r] = value
    input_sum = Scatter(parts, "tp")

    def between(dqkv, grad_inner, grad_outer_t):
        moments = blend(mom_inner, grad_inner), blend(mom_outer_t, grad_outer_t)
        blocks = to_owners(sum(map(column_blocks, moments), []))
        return input_terms(rest, dqkv), moments, blocks

    terms, (moment_inner, moment_outer_t), blocks = step(
        [input_sum], between, dqkv, grad_inner, grad_outer_t
    )
    grad_inner = grad_inner.astype(F32)
    for r, value in zip(rest, terms):
        parts[r] = value
    owners = Once(swapped(blocks))
    grad_outer, moment_outer = step([input_sum, owners], turned_moment, grad_outer_t, mom_outer)
    homes = [
        (p * tp + t, (t * (group // tp) + p // tp) * tp + (t - p % tp) % tp)
        for p in range(group)
        for t in range(tp)
    ]
    iterate = step([input_sum], orthogonal_start, owners.got[0])
    for _ in range(tp - 4):
        step([input_sum])
    iterate, grad_attn = lax.optimization_barrier((iterate, grad_attn))
    piece = Once(along(grad_attn[:, 3 * local :], (*WEIGHT_AXES, "tp"), homes))
    grad_qkv, sums = step([piece], lambda *values: values, grad_attn[:, : 3 * local], sums)
    totals = jnp.sum(lax.all_gather(sums, (*WEIGHT_AXES, "tp"), axis=0), axis=0)
    for _ in range(tp - 4):
        step([input_sum])
    own_input = Gather((grad_one + input_sum.total()).astype(BF16), "tp")

    grad_query, grad_key, grad_value = jnp.split(grad_qkv.astype(F32), 3, axis=1)
    grad_out_t = row_major(piece.got[0]).astype(F32)
    moment_query = blend(mom_query, grad_query)
    moment_key = blend(mom_key, grad_key)
    moment_value = blend(mom_value, grad_value)
    moment_out_t = blend(mom_out_t, grad_out_t)
    moments = moment_query, moment_key, moment_value, moment_out_t
    shard = lax.axis_size("shard")
    at_shard = lax.axis_index("shard")
    blocks = [row_major(m.astype(BF16)) for m in sum(map(column_blocks, moments), [])]
    blocks = row_major(jnp.stack(blocks))
    blocks = blocks.reshape(shard, -1, *blocks.shape[1:])

    def turned(value, r):
        return lax.dynamic_index_in_dim(value, lax.rem(at_shard + r, shard), 0, keepdims=False)

    owners = Exchange([turned(blocks, r)[0] for r in range(shard)], "shard")
    finish = functools.partial(orthogonal_end, group=group)
    step([owners])
    mine = row_major(jnp.stack(owners.slots))
    peers = Once(
        *[along(mine, "ctx", [(i, (i + by) % ctx) for i in range(ctx)]) for by in range(1, ctx)]
    )
    done = step([own_input, peers], finish, iterate)
    owned = jnp.concatenate([mine, *peers.got], axis=0)

    def update_ffn(back):
        half = moment_inner.shape[1] // BW
        ortho = from_owners(back, 2 * half)
        return (
            w_inner - MATRIX_RATE * jnp.concatenate(ortho[:half], axis=1),
            turned_update(back, half, group // (2 * half), w_outer),
        )

    ortho = Once(swapped(done))
    iterate = step([own_input, ortho], orthogonal_start, owned)
    done = row_major(step([own_input], finish, iterate))
    for _ in range(tp - 4):
        step([own_input])
    attn = Once(
        *[
            along(done[r], "shard", [(i, (i - r) % shard) for i in range(shard)])
            for r in range(1, shard)
        ]
    )

    def closing(back, *slots):
        return update_ffn(back), placed(slots, F32, me)

    (new_inner, new_outer), input_grad = step([attn], closing, ortho.got[0], *own_input.terms())
    input_grad = input_grad[None]
    ortho = row_major(jnp.stack([done[0], *map(row_major, attn.got)]))
    ortho = [
        lax.dynamic_index_in_dim(ortho, lax.rem(b - at_shard + shard, shard), 0, keepdims=False)
        for b in range(shard)
    ]
    ortho = [row_major(block).astype(F32) for block in ortho]
    gain_grad, bias_grad = totals[:2], totals[2:]
    new_query = w_query - MATRIX_RATE * ortho[0]
    new_key = w_key - MATRIX_RATE * ortho[1]
    new_value = w_value - MATRIX_RATE * ortho[2]
    new_out = w_out - MATRIX_RATE * ortho[3].T

    tokens_all = length * lax.axis_size("shard") * ctx
    gain_moment_new = blend(gain_moment, gain_grad)
    bias_moment_new = blend(bias_moment, bias_grad)
    new_gains = norm_gains - VECTOR_RATE * gain_moment_new / math.sqrt(tokens_all)
    new_biases = norm_biases - VECTOR_RATE * bias_moment_new / math.sqrt(tokens_all)
    return (
        layer_out,
        input_grad,
        grad_query,
        grad_key,
        grad_value,
        grad_out_t.T,
        grad_inner,
        grad_outer,
        gain_grad,
        bias_grad,
        moment_query,
        moment_key,
        moment_value,
        moment_out_t.T,
        moment_inner,
        moment_outer,
        gain_moment_new,
        bias_moment_new,
        new_query,
        new_key,
        new_value,
        new_out,
        new_inner,
        new_outer,
        new_gains,
        new_biases,
    )


def solution(mesh):
    tokens = P("shard", "ctx", None)
    by_rows = P(WEIGHT_AXES, "tp")
    by_columns = P("tp", WEIGHT_AXES)
    matrices = (by_rows, by_rows, by_rows, by_columns, by_rows, by_columns)
    return jax.shard_map(
        body,
        mesh=mesh,
        in_specs=(tokens, P(None, "shard", "ctx"), tokens, *matrices, P(), P(), *matrices, P(), P()),
        out_specs=(tokens, tokens, *matrices, P(), P(), *matrices, P(), P(), *matrices, P(), P()),
        check_vma=False,
    )
```

```python
import functools
import math

import jax
import jax.numpy as jnp
from jax import lax
from jax.experimental import pallas as pl
from jax.experimental.layout import Layout, with_layout_constraint
from jax.experimental.pallas import tpu as pltpu
from jax.sharding import PartitionSpec as P

HEAD_DIM = 128
REACH = 512
BW = 512
NS_STEPS = 5
QUERY_ROWS = 256

NS_COEFFS = (3.4445, -4.775, 2.0315)
LN_EPSILON = 1e-12
BETA = 0.5
MATRIX_RATE = 0.5
VECTOR_RATE = 0.3
MASKED = -1e30
WEIGHT_AXES = ("shard", "ctx")
BF16 = jnp.bfloat16
F32 = jnp.float32


def along(value, axis, pairs):
    return value, functools.partial(lax.ppermute, axis_name=axis, perm=pairs)


def upward(first, last):
    return [(i, i + 1) for i in range(first, last)]


def downward(first, last):
    return [(i, i - 1) for i in range(first, last)]


class Gather:
    def __init__(self, block, axis):
        self.count, self.axis = lax.axis_size(axis), axis
        self.block, self.ups, self.downs = block, [], []

    def sends(self):
        step = len(self.ups) + 1
        up, down = (self.ups[-1], self.downs[-1]) if self.ups else (self.block, self.block)
        return [
            along(up, self.axis, upward(step - 1, self.count - 1)),
            along(down, self.axis, downward(1, self.count - step + 1)),
        ]

    def take(self, got):
        self.ups.append(got[0])
        self.downs.append(got[1])

    def slot(self, r):
        return self.ups[r - 1] + self.downs[self.count - r - 1] if r else self.block

    def slots(self):
        return [self.slot(r) for r in range(self.count)]

    def terms(self):
        pairs = [[self.ups[r - 1], self.downs[self.count - r - 1]] for r in range(1, self.count)]
        return [[self.block], *pairs]


class Scatter:
    def __init__(self, parts, axis):
        self.count, self.axis = lax.axis_size(axis), axis
        self.parts, self.step, self.got = parts, 0, None

    def sends(self):
        self.step += 1
        step, count = self.step, self.count
        terms = [self.parts[step], self.parts[count - step]]
        if self.got:
            terms = [
                term.astype(F32) + got.astype(F32) for term, got in zip(terms, self.got)
            ]
        return [
            along(terms[0].astype(BF16), self.axis, upward(0, step)),
            along(terms[1].astype(BF16), self.axis, downward(count - step, count)),
        ]

    def take(self, got):
        self.got = got

    def total(self):
        return self.parts[0].astype(F32) + (self.got[0].astype(F32) + self.got[1].astype(F32))


class Exchange:
    def __init__(self, blocks, axis):
        self.blocks, self.axis = blocks, axis

    def sends(self):
        count = len(self.blocks)
        return [
            along(self.blocks[r], self.axis, [(i, (i + r) % count) for i in range(count)])
            for r in range(1, count)
        ]

    def take(self, got):
        self.slots = [self.blocks[0], *got]


class Once:
    def __init__(self, *sends):
        self.all = list(sends)

    def sends(self):
        return self.all

    def take(self, got):
        self.got = got


def step(movers, work=None, *operands):
    sends = [mover.sends() for mover in movers]
    values = [[value for value, _ in group] for group in sends]
    values, operands = lax.optimization_barrier((values, operands))
    got = [
        [send(value) for value, (_, send) in zip(vals, group)] for vals, group in zip(values, sends)
    ]
    done = work(*operands) if work else ()
    got, done = lax.optimization_barrier((got, done))
    for mover, arrived in zip(movers, got):
        mover.take(arrived)
    return done


def slot_order(count):
    order = []
    for hop in range(1, count):
        order += [r for r in dict.fromkeys((hop, count - hop)) if r not in order]
    return order + [0]


def after(value, *others):
    return lax.optimization_barrier((value, *others))[0]


def row_major(value):
    return with_layout_constraint(value, Layout(major_to_minor=tuple(range(value.ndim))))


def dot(left, right):
    return jnp.dot(left, right, preferred_element_type=F32)


def dot_nt(left, right):
    return lax.dot_general(left, right, (((1,), (1,)), ((), ())), preferred_element_type=F32)


def dot_tn(left, right):
    return lax.dot_general(left, right, (((0,), (0,)), ((), ())), preferred_element_type=F32)


def normalize(hidden):
    centred = hidden - jnp.mean(hidden, axis=-1, keepdims=True)
    variance = jnp.mean(centred * centred, axis=-1, keepdims=True)
    scale = lax.rsqrt(variance + LN_EPSILON)
    return centred * scale, scale


def norm_backward(grad, unit, scale, gain):
    scaled = grad * gain
    inner = jnp.mean(scaled * unit, axis=-1, keepdims=True)
    dhidden = scale * (scaled - jnp.mean(scaled, axis=-1, keepdims=True) - unit * inner)
    return dhidden, jnp.sum(grad * unit, axis=0), jnp.sum(grad, axis=0)


def gelu_tanh(values):
    return jax.nn.gelu(values, approximate=True)


def window_probs(q, keys, low_ref, high_ref, start):
    scores = dot_nt(keys, q) * (HEAD_DIM**-0.5)
    at = start + lax.broadcasted_iota(jnp.int32, scores.shape, 0)
    scores = jnp.where((at >= low_ref[...]) & (at <= high_ref[...]), scores, MASKED)
    expo = jnp.exp(scores - jnp.max(scores, axis=0, keepdims=True))
    return expo * (1.0 / jnp.sum(expo, axis=0, keepdims=True))


def attend_kernel(low_ref, high_ref, q_ref, k_ref, v_ref, o_ref):
    rows = q_ref.shape[0]
    span = rows + 2 * REACH
    start = pl.multiple_of(pl.program_id(1) * rows, rows)
    probs = window_probs(q_ref[...], k_ref[pl.ds(start, span), :], low_ref, high_ref, start)
    o_ref[...] = dot_tn(probs.astype(BF16), v_ref[pl.ds(start, span), :]).astype(BF16)


def attend_back_kernel(
    low_ref, high_ref, q_ref, k_ref, v_ref, g_ref, dq_ref, above_ref, centre_ref, below_ref, total
):
    rows = q_ref.shape[0]
    span = rows + 2 * REACH
    start = pl.multiple_of(pl.program_id(1) * rows, rows)
    window = pl.ds(start, span)

    @pl.when(pl.program_id(1) == 0)
    def _():
        total[...] = jnp.zeros_like(total)

    q, g, keys = q_ref[...], g_ref[...], k_ref[window, :]
    probs = window_probs(q, keys, low_ref, high_ref, start)
    dprobs = dot_nt(v_ref[window, :], g)
    offset = jnp.sum(dprobs * probs, axis=0, keepdims=True)
    dscores = (probs * (dprobs - offset) * (HEAD_DIM**-0.5)).astype(BF16)
    total[1, window, :] += dot(probs.astype(BF16), g)
    total[0, window, :] += dot(dscores, q)
    dq_ref[...] = dot_tn(dscores, keys).astype(BF16)

    @pl.when(pl.program_id(1) == pl.num_programs(1) - 1)
    def _():
        length = centre_ref.shape[1]
        above_ref[...] = total[:, :REACH, :].astype(BF16)
        centre_ref[...] = total[:, REACH : REACH + length, :]
        below_ref[...] = total[:, REACH + length :, :].astype(BF16)


def attention_specs(rows, padded, heads):
    bounds = pl.BlockSpec((1, rows), lambda h, b: (0, b))
    queries = pl.BlockSpec((rows, HEAD_DIM), lambda h, b: (b, h))
    keys = pl.BlockSpec((padded, HEAD_DIM), lambda h, b: (0, h))
    values = pl.BlockSpec((padded, HEAD_DIM), lambda h, b: (0, h + heads))
    return bounds, queries, keys, values


def attend(low, high, qkv, padded_kv, heads):
    length, padded = qkv.shape[0], padded_kv.shape[0]
    rows = min(QUERY_ROWS, length)
    bounds, q_spec, k_spec, v_spec = attention_specs(rows, padded, heads)
    pairs = heads * length * (rows + 2 * REACH)
    return pl.pallas_call(
        attend_kernel,
        grid=(heads, length // rows),
        in_specs=[bounds, bounds, q_spec, k_spec, v_spec],
        out_specs=q_spec,
        out_shape=jax.ShapeDtypeStruct((length, heads * HEAD_DIM), BF16),
        cost_estimate=pl.CostEstimate(
            flops=16 * pairs * HEAD_DIM, transcendentals=pairs, bytes_accessed=8 << 20
        ),
        name="attend",
    )(low, high, qkv, padded_kv, padded_kv)


def attend_back(low, high, qkv, padded_kv, grads, heads):
    length, padded = qkv.shape[0], padded_kv.shape[0]
    rows = min(QUERY_ROWS, length)
    bounds, q_spec, k_spec, v_spec = attention_specs(rows, padded, heads)
    pairs = heads * length * (rows + 2 * REACH)
    width = heads * HEAD_DIM

    def stacked(count):
        return pl.BlockSpec((2, count, HEAD_DIM), lambda h, b: (0, 0, h))

    return pl.pallas_call(
        attend_back_kernel,
        grid=(heads, length // rows),
        in_specs=[bounds, bounds, q_spec, k_spec, v_spec, q_spec],
        out_specs=(q_spec, stacked(REACH), stacked(length), stacked(REACH)),
        out_shape=(
            jax.ShapeDtypeStruct((length, width), BF16),
            jax.ShapeDtypeStruct((2, REACH, width), BF16),
            jax.ShapeDtypeStruct((2, length, width), F32),
            jax.ShapeDtypeStruct((2, REACH, width), BF16),
        ),
        scratch_shapes=[pltpu.VMEM((2, padded, HEAD_DIM), F32)],
        cost_estimate=pl.CostEstimate(
            flops=32 * pairs * HEAD_DIM, transcendentals=pairs, bytes_accessed=20 << 20
        ),
        name="attend_back",
    )(low, high, qkv, padded_kv, padded_kv, grads)


def place_kernel(sizes, me_ref, *refs):
    at = 0
    for r, size in enumerate(sizes):
        terms = refs[at : at + size]
        at += size

        @pl.when(pl.program_id(0) == r)
        def _(terms=terms):
            value = terms[0][...]
            for term in terms[1:]:
                value = value + term[...]
            refs[-1][...] = value.astype(refs[-1].dtype)


def placed(slots, dtype, me):
    count = len(slots)
    share, width = slots[0][0].shape
    flat = [term for slot in slots for term in slot]
    whole = pl.BlockSpec((share, width), lambda r, me_ref: (0, 0))
    return pl.pallas_call(
        functools.partial(place_kernel, [len(slot) for slot in slots]),
        grid_spec=pltpu.PrefetchScalarGridSpec(
            num_scalar_prefetch=1,
            grid=(count,),
            in_specs=[whole] * len(flat),
            out_specs=pl.BlockSpec(
                (share, width), lambda r, me_ref: (lax.rem(me_ref[0] - r + count, count), 0)
            ),
        ),
        out_shape=jax.ShapeDtypeStruct((count * share, width), dtype),
        cost_estimate=pl.CostEstimate(
            flops=0, transcendentals=0, bytes_accessed=6 * count * share * width
        ),
        name="place",
    )(me.reshape(1), *flat)


def halves(value):
    top = value.astype(BF16)
    return top, (value - top.astype(F32)).astype(BF16)


def newton_schulz_kernel(steps, in_ref, out_ref, top, rest, iterate=None):
    opening = iterate is None
    iterate = out_ref if opening else iterate
    depth = top.shape[1]
    chunk = min(1024, depth)
    chunks = depth // chunk

    def columns(c):
        return pl.ds(pl.multiple_of(c * chunk, chunk), chunk)

    def load(c, total):
        part = in_ref[columns(c), :].astype(F32)
        iterate[:, columns(c)] = part.T
        return total + jnp.sum(part * part, axis=(0, 1), keepdims=True)

    if opening:
        norm = jnp.sqrt(lax.fori_loop(0, chunks, load, jnp.zeros((1, 1), F32)))
        inverse = 1.0 / (norm + 1e-07)

    def split(c, carry):
        value = iterate[:, columns(c)] * inverse if opening else in_ref[:, columns(c)]
        iterate[:, columns(c)] = value
        top[:, columns(c)], rest[:, columns(c)] = halves(value)
        return carry

    lax.fori_loop(0, chunks, split, 0)

    def step(index, carry):
        gram = dot_nt(top[...], top[...])
        gram_top, gram_rest = halves(gram)
        cross = dot(gram_top, gram_rest)
        square = dot(gram_top, gram_top) + (cross + cross.T)
        poly_top, poly_rest = halves(NS_COEFFS[1] * gram + NS_COEFFS[2] * square)

        def update(c, carry):
            here = columns(c)
            change = dot(poly_top, top[:, here]) + dot(poly_rest, top[:, here])
            value = NS_COEFFS[0] * iterate[:, here] + (change + dot(poly_top, rest[:, here]))
            iterate[:, here] = value
            top[:, here], rest[:, here] = halves(value)
            return carry

        return lax.fori_loop(0, chunks, update, carry)

    lax.fori_loop(0, steps, step, 0)

    def store(c, carry):
        out_ref[columns(c), :] = iterate[:, columns(c)].T.astype(BF16)
        return carry

    if not opening:
        lax.fori_loop(0, chunks, store, 0)


def newton_schulz_part(steps, value, out, depth, width, scratch):
    return pl.pallas_call(
        functools.partial(newton_schulz_kernel, steps),
        out_shape=out,
        in_specs=[pl.BlockSpec(memory_space=pltpu.VMEM)],
        out_specs=pl.BlockSpec(memory_space=pltpu.VMEM),
        scratch_shapes=[pltpu.VMEM((width, depth), BF16), pltpu.VMEM((width, depth), BF16), *scratch],
        cost_estimate=pl.CostEstimate(
            flops=2 * steps * width * width * (4 * depth + 2 * width),
            transcendentals=0,
            bytes_accessed=6 * depth * width,
        ),
        name="newton_schulz",
    )(value)


def orthogonal_start(owned):
    depth, width = owned.shape[0] * owned.shape[1], owned.shape[2]
    out = jax.ShapeDtypeStruct((width, depth), F32)
    return newton_schulz_part(NS_STEPS // 2, owned.reshape(depth, width), out, depth, width, [])


def orthogonal_end(iterate, group):
    width, depth = iterate.shape
    out = jax.ShapeDtypeStruct((depth, width), BF16)
    scratch = [pltpu.VMEM((width, depth), F32)]
    done = newton_schulz_part(NS_STEPS - NS_STEPS // 2, iterate, out, depth, width, scratch)
    return done.reshape(group, depth // group, width)


def to_owners(blocks):
    copies = lax.axis_size("shard") * lax.axis_size("ctx") // len(blocks)
    return jnp.stack([block.astype(BF16) for block in blocks for _ in range(copies)])


def swapped(value):
    return value, functools.partial(
        lax.all_to_all, axis_name=WEIGHT_AXES, split_axis=0, concat_axis=0, tiled=True
    )


def from_owners(back, count):
    copies = back.shape[0] // count
    return [back[b * copies].astype(F32) for b in range(count)]


def column_blocks(value):
    return [value[:, at : at + BW] for at in range(0, value.shape[1], BW)]


def turn_kernel(grad_ref, old_ref, out_ref, moment_ref):
    turned = grad_ref[...].astype(F32).T
    out_ref[...] = turned
    moment_ref[...] = BETA * old_ref[...] + (1.0 - BETA) * turned


def turned_moment(grad_t, old):
    rows, width = grad_t.shape
    here = pl.BlockSpec((BW, rows), lambda j: (j, 0))
    out = jax.ShapeDtypeStruct((width, rows), F32)
    return pl.pallas_call(
        turn_kernel,
        grid=(width // BW,),
        in_specs=[pl.BlockSpec((rows, BW), lambda j: (0, j)), here],
        out_specs=(here, here),
        out_shape=(out, out),
        cost_estimate=pl.CostEstimate(
            flops=3 * rows * width, transcendentals=0, bytes_accessed=14 * rows * width
        ),
        name="turn",
    )(grad_t, old)


def update_kernel(ortho_ref, old_ref, out_ref):
    out_ref[...] = old_ref[...] - MATRIX_RATE * ortho_ref[...].astype(F32).T


def turned_update(back, first, copies, old):
    width, rows = old.shape
    here = pl.BlockSpec((BW, rows), lambda j: (j, 0))
    return pl.pallas_call(
        update_kernel,
        grid=(width // BW,),
        in_specs=[pl.BlockSpec((None, rows, BW), lambda j: ((first + j) * copies, 0, 0)), here],
        out_specs=here,
        out_shape=jax.ShapeDtypeStruct((width, rows), F32),
        cost_estimate=pl.CostEstimate(
            flops=2 * rows * width, transcendentals=0, bytes_accessed=10 * rows * width
        ),
        name="update",
    )(back, old)


def gather_rows(value):
    return lax.all_gather(value, WEIGHT_AXES, axis=0, tiled=True)


def scatter_rows(value):
    return lax.psum_scatter(value, WEIGHT_AXES, scatter_dimension=0, tiled=True)


def blend(old, grad):
    return BETA * old + (1.0 - BETA) * grad


def body(
    hidden_in,
    doc_span,
    cotangent,
    w_query,
    w_key,
    w_value,
    w_out,
    w_inner,
    w_outer,
    norm_gains,
    norm_biases,
    mom_query,
    mom_key,
    mom_value,
    mom_out,
    mom_inner,
    mom_outer,
    gain_moment,
    bias_moment,
):
    tp = lax.axis_size("tp")
    me = lax.axis_index("tp")
    hidden = hidden_in[0]
    length, width = hidden.shape
    share = length // tp
    local = w_query.shape[1]
    heads = local // HEAD_DIM

    def slice_of(value, r):
        return lax.dynamic_slice_in_dim(value, lax.rem(me - r + tp, tp) * share, share, 0)

    full_qkv = gather_rows(jnp.concatenate([w_query, w_key, w_value], axis=1).astype(BF16))
    w_out_t = Gather(w_out.T.astype(BF16), "tp")
    for _ in range(tp - 1):
        step([w_out_t])
    full_out_t = gather_rows(jnp.concatenate(w_out_t.slots(), axis=1))
    full_inner = gather_rows(w_inner.astype(BF16))
    full_outer_t = gather_rows(w_outer.T.astype(BF16))

    qkv = dot(hidden, full_qkv).astype(BF16)
    own_kv = qkv[:, local:]
    ctx = lax.axis_size("ctx")
    edges = Once(
        along(own_kv[length - REACH :], "ctx", upward(0, ctx - 1)),
        along(own_kv[:REACH], "ctx", downward(1, ctx)),
    )
    step([edges])
    padded_kv = jnp.concatenate([edges.got[0], own_kv, edges.got[1]], axis=0)

    position = jnp.arange(length, dtype=jnp.int32)
    anchor = lax.axis_index("ctx") * length - REACH
    low = jnp.maximum(doc_span[0] - anchor, position[None])
    high = jnp.minimum(doc_span[1] - anchor, position[None] + 2 * REACH)
    attended = attend(low, high, qkv, padded_kv, heads)

    all_heads = Gather(attended, "tp")
    mom_outer_t, mom_out_t = step([all_heads], lambda a, b: (a.T, b.T), mom_outer, mom_out)
    for _ in range(tp - 2):
        step([all_heads])
    head_slots = all_heads.slots()

    order = slot_order(tp)
    first, rest = order[:2], order[2:]
    normed_slots, pre_slots, act_slots, parts = ([None] * tp for _ in range(4))
    def forward(r):
        attended_r = jnp.concatenate([slice_of(slot, r) for slot in head_slots], axis=1)
        branch = dot_nt(attended_r, full_out_t)
        unit, scale = normalize(slice_of(hidden, r).astype(F32) + branch)
        normed = unit * norm_gains[0] + norm_biases[0]
        normed_slots[r] = normed.astype(BF16)
        pre_slots[r] = dot(normed_slots[r], full_inner)
        act_slots[r] = gelu_tanh(pre_slots[r]).astype(BF16)
        return unit, scale, normed

    def terms_of(slots, *acts):
        return [
            dot_nt(act, full_outer_t).astype(F32 if r == 0 else BF16) for r, act in zip(slots, acts)
        ]

    for r in order:
        unit_one, scale_one, own_normed = forward(r)
    for r, value in zip(first, terms_of(first, *[act_slots[r] for r in first])):
        parts[r] = value
    ffn_sum = Scatter(parts, "tp")
    acts = [act_slots[r] for r in rest]
    for r, value in zip(rest, step([ffn_sum], functools.partial(terms_of, rest), *acts)):
        parts[r] = value

    def slopes_of(*pres):
        return [jax.vjp(gelu_tanh, pre)[1](jnp.ones_like(pre))[0] for pre in pres]

    slopes = [None] * tp
    half = tp // 2
    slopes[:half] = step([ffn_sum], slopes_of, *pre_slots[:half])
    slopes[half:] = step([ffn_sum], slopes_of, *pre_slots[half:])
    for _ in range(tp - 4):
        step([ffn_sum])

    unit_two, scale_two = normalize(own_normed + ffn_sum.total())
    own_out = (unit_two * norm_gains[1] + norm_biases[1]).astype(BF16)
    seed = slice_of(cotangent[0], 0).astype(F32)
    grad_two, gain_two, shift_two = norm_backward(seed, unit_two, scale_two, norm_gains[1])
    dffn_all = Gather(grad_two.astype(BF16), "tp")
    dpre_slots, parts = [None] * tp, [None] * tp

    def backward(*pairs):
        made = []
        for dffn, slope in pairs:
            dpre = (dot(dffn, full_outer_t) * slope).astype(BF16)
            made.append((dpre, dot_nt(dpre, full_inner).astype(BF16)))
        return made

    def keep_back(slots, made):
        for r, values in zip(slots, made):
            dpre_slots[r], parts[r] = values

    step([dffn_all])
    keep_back([0], step([dffn_all], backward, (dffn_all.slot(0), slopes[0])))
    middle = [r for r in rest if r]
    ready = [(dffn_all.slot(r), slopes[r]) for r in middle] if tp == 4 else []
    made = step([dffn_all], backward, *ready)
    for _ in range(tp - 4):
        step([dffn_all])
    if not ready:
        made = backward(*[(dffn_all.slot(r), slopes[r]) for r in middle])
    keep_back(middle, made)
    dffn_slots = dffn_all.slots()
    out_all = Gather(own_out, "tp")
    keep_back(first, step([out_all], backward, *[(dffn_slots[r], slopes[r]) for r in first]))

    dnormed_sum = Scatter(parts, "tp")

    def weight_grad(lefts, rights):
        return dot_tn(jnp.concatenate(lefts, axis=0), jnp.concatenate(rights, axis=0)).astype(BF16)

    grad_outer_t = step([out_all, dnormed_sum], weight_grad, dffn_slots, act_slots)
    grad_outer_t = scatter_rows(grad_outer_t)
    grad_inner = step([out_all, dnormed_sum], weight_grad, normed_slots, dpre_slots)
    grad_inner = scatter_rows(grad_inner)
    layer_out = step([dnormed_sum], lambda *slots: placed(slots, BF16, me), *out_all.terms())[None]
    for _ in range(tp - 4):
        step([dnormed_sum])
    dnormed = grad_two + dnormed_sum.total()

    grad_one, gain_one, shift_one = norm_backward(dnormed, unit_one, scale_one, norm_gains[0])
    dbranch_low = grad_one.astype(BF16)
    dattended_all = dot(dbranch_low, full_out_t).astype(BF16)
    blocks = [dattended_all[:, (-r % tp) * local : (-r % tp + 1) * local] for r in range(tp)]
    dattended = Exchange(blocks, "tp")
    sums = jnp.stack([gain_one, gain_two, shift_one, shift_two])
    step([dattended])
    part = width // tp
    dbranch = Exchange(
        [
            lax.dynamic_slice_in_dim(dbranch_low, lax.rem(me + r, tp) * part, part, 1)
            for r in range(tp)
        ],
        "tp",
    )

    def attention_back(*slots):
        return attend_back(low, high, qkv, padded_kv, placed([[slot] for slot in slots], BF16, me), heads)

    dq_low, kv_above, kv_centre, kv_below = step([dbranch], attention_back, *dattended.slots)
    edges = Once(
        along(kv_above, "ctx", downward(1, ctx)), along(kv_below, "ctx", upward(0, ctx - 1))
    )
    rows = w_query.shape[0]
    group = width // rows

    def out_pieces(dbranch_slots, head_slots):
        columns = placed([[slot] for slot in dbranch_slots], BF16, me)
        sums = [dot_tn(columns, slot).astype(BF16).reshape(-1, rows, local) for slot in head_slots]
        sums = jnp.stack(sums, axis=1).reshape(group * rows, local)
        return row_major(jnp.pad(sums, ((0, 0), (3 * local, 0))))

    pieces = step([edges], out_pieces, dbranch.slots, head_slots)
    from_above, from_below = (edge.astype(F32) for edge in edges.got)
    beyond = length - REACH
    added = jnp.pad(from_above, ((0, 0), (beyond, 0), (0, 0))) + jnp.pad(
        from_below, ((0, 0), (0, beyond), (0, 0))
    )
    kv_low = (kv_centre + added).astype(BF16)
    dqkv = jnp.concatenate([dq_low, kv_low[0], kv_low[1]], axis=1)
    grad_qkv = dot_tn(hidden, dqkv).astype(BF16)
    grad_attn = row_major(lax.dynamic_update_slice(pieces, grad_qkv, (0, 0)))
    dqkv = after(dqkv, grad_attn)
    grad_attn = scatter_rows(grad_attn)

    parts = [None] * tp

    def input_terms(slots, dqkv):
        rows = jnp.concatenate([slice_of(dqkv, r) for r in slots], axis=0)
        sums = dot_nt(rows, full_qkv).astype(BF16)
        return [sums[n * share : (n + 1) * share] for n in range(len(slots))]

    for r, value in zip(first, input_terms(first, dqkv)):
        parts[r] = value
    input_sum = Scatter(parts, "tp")

    def between(dqkv, grad_inner, grad_outer_t):
        moments = blend(mom_inner, grad_inner), blend(mom_outer_t, grad_outer_t)
        blocks = to_owners(sum(map(column_blocks, moments), []))
        return input_terms(rest, dqkv), moments, blocks

    terms, (moment_inner, moment_outer_t), blocks = step(
        [input_sum], between, dqkv, grad_inner, grad_outer_t
    )
    grad_inner = grad_inner.astype(F32)
    for r, value in zip(rest, terms):
        parts[r] = value
    owners = Once(swapped(blocks))
    grad_outer, moment_outer = step([input_sum, owners], turned_moment, grad_outer_t, mom_outer)
    homes = [
        (p * tp + t, (t * (group // tp) + p // tp) * tp + (t - p % tp) % tp)
        for p in range(group)
        for t in range(tp)
    ]
    iterate = step([input_sum], orthogonal_start, owners.got[0])
    for _ in range(tp - 4):
        step([input_sum])
    iterate, grad_attn = lax.optimization_barrier((iterate, grad_attn))
    piece = Once(along(grad_attn[:, 3 * local :], (*WEIGHT_AXES, "tp"), homes))
    grad_qkv, sums = step([piece], lambda *values: values, grad_attn[:, : 3 * local], sums)
    totals = jnp.sum(lax.all_gather(sums, (*WEIGHT_AXES, "tp"), axis=0), axis=0)
    for _ in range(tp - 4):
        step([input_sum])
    own_input = Gather((grad_one + input_sum.total()).astype(BF16), "tp")

    grad_query, grad_key, grad_value = jnp.split(grad_qkv.astype(F32), 3, axis=1)
    grad_out_t = row_major(piece.got[0]).astype(F32)
    moment_query = blend(mom_query, grad_query)
    moment_key = blend(mom_key, grad_key)
    moment_value = blend(mom_value, grad_value)
    moment_out_t = blend(mom_out_t, grad_out_t)
    moments = moment_query, moment_key, moment_value, moment_out_t
    shard = lax.axis_size("shard")
    at_shard = lax.axis_index("shard")
    blocks = [row_major(m.astype(BF16)) for m in sum(map(column_blocks, moments), [])]
    blocks = row_major(jnp.stack(blocks))
    blocks = blocks.reshape(shard, -1, *blocks.shape[1:])

    def turned(value, r):
        return lax.dynamic_index_in_dim(value, lax.rem(at_shard + r, shard), 0, keepdims=False)

    owners = Exchange([turned(blocks, r)[0] for r in range(shard)], "shard")
    finish = functools.partial(orthogonal_end, group=group)
    step([owners])
    mine = row_major(jnp.stack(owners.slots))
    peers = Once(
        *[along(mine, "ctx", [(i, (i + by) % ctx) for i in range(ctx)]) for by in range(1, ctx)]
    )
    done = step([own_input, peers], finish, iterate)
    owned = jnp.concatenate([mine, *peers.got], axis=0)

    def update_ffn(back):
        half = moment_inner.shape[1] // BW
        ortho = from_owners(back, 2 * half)
        return (
            w_inner - MATRIX_RATE * jnp.concatenate(ortho[:half], axis=1),
            turned_update(back, half, group // (2 * half), w_outer),
        )

    ortho = Once(swapped(done))
    iterate = step([own_input, ortho], orthogonal_start, owned)
    done = row_major(step([own_input], finish, iterate))
    for _ in range(tp - 4):
        step([own_input])
    attn = Once(
        *[
            along(done[r], "shard", [(i, (i - r) % shard) for i in range(shard)])
            for r in range(1, shard)
        ]
    )

    def closing(back, *slots):
        return update_ffn(back), placed(slots, F32, me)

    (new_inner, new_outer), input_grad = step([attn], closing, ortho.got[0], *own_input.terms())
    input_grad = input_grad[None]
    ortho = row_major(jnp.stack([done[0], *map(row_major, attn.got)]))
    ortho = [
        lax.dynamic_index_in_dim(ortho, lax.rem(b - at_shard + shard, shard), 0, keepdims=False)
        for b in range(shard)
    ]
    ortho = [row_major(block).astype(F32) for block in ortho]
    gain_grad, bias_grad = totals[:2], totals[2:]
    new_query = w_query - MATRIX_RATE * ortho[0]
    new_key = w_key - MATRIX_RATE * ortho[1]
    new_value = w_value - MATRIX_RATE * ortho[2]
    new_out = w_out - MATRIX_RATE * ortho[3].T

    tokens_all = length * lax.axis_size("shard") * ctx
    gain_moment_new = blend(gain_moment, gain_grad)
    bias_moment_new = blend(bias_moment, bias_grad)
    new_gains = norm_gains - VECTOR_RATE * gain_moment_new / math.sqrt(tokens_all)
    new_biases = norm_biases - VECTOR_RATE * bias_moment_new / math.sqrt(tokens_all)
    return (
        layer_out,
        input_grad,
        grad_query,
        grad_key,
        grad_value,
        grad_out_t.T,
        grad_inner,
        grad_outer,
        gain_grad,
        bias_grad,
        moment_query,
        moment_key,
        moment_value,
        moment_out_t.T,
        moment_inner,
        moment_outer,
        gain_moment_new,
        bias_moment_new,
        new_query,
        new_key,
        new_value,
        new_out,
        new_inner,
        new_outer,
        new_gains,
        new_biases,
    )


def solution(mesh):
    tokens = P("shard", "ctx", None)
    by_rows = P(WEIGHT_AXES, "tp")
    by_columns = P("tp", WEIGHT_AXES)
    matrices = (by_rows, by_rows, by_rows, by_columns, by_rows, by_columns)
    return jax.shard_map(
        body,
        mesh=mesh,
        in_specs=(tokens, P(None, "shard", "ctx"), tokens, *matrices, P(), P(), *matrices, P(), P()),
        out_specs=(tokens, tokens, *matrices, P(), P(), *matrices, P(), P(), *matrices, P(), P()),
        check_vma=False,
    )
```
